32 devices in a mesh: row: 4 (over z), col: 8 (over y, x, core).
Axes of the slice: x: 2, y: 2, z: 4, core: 2. Of those that a mesh axis runs over, the one named last changes fastest.
Arguments:
- activations: bfloat16 [4096, 8192], P('row', 'col'), may hold values from -6 to 6
- errors: bfloat16 [4096, 8192], P('row', 'col'), may hold values from -6 to 6
- act_proj: bfloat16 [8192, 128], P('col'), may hold values from -0.0625 to 0.0625
- err_proj: bfloat16 [8192, 128], P('col'), may hold values from -0.0625 to 0.0625
- lengths: int32 [4, 64], P('row'), may hold values from 1 to 256, 1024 in all within a row
- ridge: float32 [16384, 16384], P('row', 'col'), may hold values from -4 to 36, as said below
- pivot_inverse: float32 [2, 512, 512], replicated, may hold values from -1 to 1
Outputs:
- eliminated: float32 [16384, 16384], P('row', 'col')
The draws below stay inside these ranges and needn't reach their ends.
Inputs may be any that keep to these rules, and one draw needn't show every extreme that they name: The lengths of one row group sum to 1024. `ridge`: Symmetric.
All inputs are finite; a program needn't handle non-finite values.
Results may differ from the reference program's by a relative error of at most 0.0074.
Values may be sent and summed in bfloat16 or wider, within the bound.
No kernel may reach another device: no remote copies, remote signals or barrier semaphores. Data moves between devices by JAX's collectives and lax.ppermute only.
A program may use at most 192 MiB of HBM per device.

```python
import math
import jax
import jax.numpy as jnp
import numpy as np
from jax import lax

D = 8192
PROJ = 128
PANEL = 512
CAP_DEV = 64
TOK_DEV = 1024
CAPTIONS = 256
TOKENS = 4096
ORDER = 16384
N_ROW = 4


def draw_ridge(key, part):
    order = PROJ * PROJ
    key_diag, key_off = jax.random.split(jax.random.fold_in(key, 11))
    diagonal = jnp.exp(jax.random.uniform(key_diag, (order,), jnp.float32, math.log(8.0), math.log(32.0)))
    uniform_part = jax.random.uniform(key_off, (order, order), jnp.float32, -1.0, 1.0)
    symmetric = 2.0 * (uniform_part + uniform_part.T)
    return symmetric + jnp.diag(diagonal)


def draw_pivot_inverse(key, part):
    key_diag, key_off = jax.random.split(jax.random.fold_in(key, 23))
    diagonal = jnp.exp(jax.random.uniform(key_diag, (2, PANEL), jnp.float32, math.log(0.06), math.log(0.15)))
    strict_lower = jax.random.truncated_normal(key_off, -4.0, 4.0, (2, PANEL, PANEL), jnp.float32) * (0.03 / math.sqrt(PANEL))
    lower_mask = jnp.tril(jnp.ones((PANEL, PANEL), jnp.float32), -1)
    return strict_lower * lower_mask[None] + diagonal[:, :, None] * jnp.eye(PANEL, dtype=jnp.float32)[None]


def level_of(rng, dims, pieces, low, top_value):
    factor_of, own = 1.0, jax.random.fold_in(rng, 6)
    for dim, parts in pieces:
        draws = jnp.exp(jax.random.uniform(jax.random.fold_in(own, dim), (parts,), jnp.float32, low / len(pieces), top_value / len(pieces)))
        factor_of = factor_of * jnp.repeat(draws, dims[dim] // parts).reshape([-1 if axis == dim else 1 for axis in range(len(dims))])
    return factor_of


def profile(count, total, most, skew):
    loads = [(1 << 20) // math.isqrt(standing ** skew) + 1 for standing in range(2, count + 1)]
    spare, holding = total - most - (count - 1), [1] * (count - 1)
    while spare > 0:
        movable = [i for i in range(count - 1) if holding[i] < most]
        whole, remaining = sum([loads[i] for i in movable]), spare
        for i in movable:
            more = min(most - holding[i], max(1, remaining * loads[i] // whole), spare)
            holding[i] = holding[i] + more
            spare = spare - more
    return np.array([most] + holding)


def ragged_sizes(own_key, amount, total, reach, skew):
    if amount == 2:
        one = jax.random.randint(own_key, (), max(1, total - reach), min(reach, total - 1) + 1)
        return jnp.stack([one, total - one])
    sizes = jnp.asarray(profile(amount, total, reach, skew), jnp.int32)
    pairs = (amount - 1) // 2
    donor, taker = sizes[1:1 + 2 * pairs:2], sizes[2:2 + 2 * pairs:2]
    margin = jnp.minimum(donor - 1, reach - taker)
    moved = jax.random.randint(jax.random.fold_in(own_key, 1), (pairs,), 0, 1 << 20) % (margin + 1)
    sizes = sizes.at[1:1 + 2 * pairs:2].set(donor - moved).at[2:2 + 2 * pairs:2].set(taker + moved)
    return sizes[jax.random.permutation(jax.random.fold_in(own_key, 2), amount)]


def noise(key, shape, scale, reach, cuts=(), kind=jnp.bfloat16):
    result = scale * jax.random.normal(key, shape, jnp.float32)
    if cuts:
        result = result * level_of(key, shape, cuts, -0.22, 0.18)
    return jnp.clip(result, -reach, reach).astype(kind)


def setup_inputs(seed: int = 0) -> dict:
    seeds = jax.random.split(jax.random.key(seed), 8)
    return {
        "activations": noise(seeds[0], (TOKENS, D), 1.0, 6.0, ((0, 4), (1, 8))),
        "errors": noise(seeds[1], (TOKENS, D), 1.0, 6.0, ((0, 4), (1, 8))),
        "act_proj": noise(seeds[2], (D, PROJ), D ** -0.5, 0.0625, ((0, 8),)),
        "err_proj": noise(seeds[3], (D, PROJ), D ** -0.5, 0.0625, ((0, 8),)),
        "lengths": jax.vmap(lambda own: ragged_sizes(own, CAP_DEV, TOK_DEV, TOK_DEV // 4, 2))(jax.random.split(seeds[4], N_ROW)).reshape((N_ROW, CAP_DEV)).astype(jnp.int32),
        "ridge": draw_ridge(jax.random.fold_in(seeds[7], 71), 0),
        "pivot_inverse": draw_pivot_inverse(jax.random.fold_in(seeds[7], 71), 0),
    }


def group_grads(inputs):
    proj_err, proj_act, lengths_row = inputs
    caption_end = jnp.cumsum(lengths_row).astype(jnp.int32)
    caption_start = (caption_end - lengths_row).astype(jnp.int32)
    positions = jnp.arange(TOK_DEV, dtype=jnp.int32)[:, None]
    member = ((positions >= caption_start[None, :]) & (positions < caption_end[None, :])).astype(jnp.float32)
    weighted = (proj_err.astype(jnp.float32)[:, :, None] * member[:, None, :]).reshape(TOK_DEV, PROJ * CAP_DEV)
    summed = jnp.dot(weighted.T, proj_act.astype(jnp.float32), precision=lax.Precision.HIGHEST)
    summed = summed.reshape(PROJ, CAP_DEV, PROJ).transpose(1, 0, 2).reshape(CAP_DEV, PROJ * PROJ)
    return summed.astype(jnp.bfloat16)


def reference(activations, errors, act_proj, err_proj, lengths, ridge, pivot_inverse):
    proj_act = jnp.dot(activations, act_proj, preferred_element_type=jnp.float32).astype(jnp.bfloat16)
    proj_err = jnp.dot(errors, err_proj, preferred_element_type=jnp.float32).astype(jnp.bfloat16)
    grads = lax.map(group_grads, (proj_err.reshape(N_ROW, TOK_DEV, PROJ), proj_act.reshape(N_ROW, TOK_DEV, PROJ), lengths))
    grads = grads.reshape(CAPTIONS, ORDER).astype(jnp.float32)
    matrix = ridge + jnp.dot(grads.T, grads, precision=lax.Precision.HIGHEST) / CAPTIONS
    row_ids = jnp.arange(ORDER, dtype=jnp.int32)[:, None]
    for panel_index in range(2):
        start_col = panel_index * PANEL
        stop_col = start_col + PANEL
        panel = jnp.dot(matrix[:, start_col:stop_col], pivot_inverse[panel_index].T, precision=lax.Precision.HIGHEST)
        panel = jnp.where(row_ids >= start_col, panel, 0.0)
        tail_rows = panel[stop_col:]
        matrix = matrix.at[stop_col:, stop_col:].add(-jnp.dot(tail_rows, tail_rows.T, precision=lax.Precision.HIGHEST))
        matrix = matrix.at[:, start_col:stop_col].set(panel)
        matrix = matrix.at[start_col:stop_col, stop_col:].set(0.0)
    return matrix
```

```python
import functools

import jax
import jax.numpy as jnp
from jax import lax
from jax.experimental import pallas as pl
from jax.experimental.pallas import tpu as pltpu
from jax.sharding import PartitionSpec as P


BF16 = jnp.bfloat16
F32 = jnp.float32
PLANE_CHUNKS = 4
LINE_CHUNKS = 8
CHAINS = 2
CALLS = ((0, 1, 2, 3), (4, 5, 6, 7))
SPLITS = (((0,), (1,)), ((0, 1),))
ROW_BLOCK = 512


def xor_pairs(count, bit):
    return [(i, i ^ bit) for i in range(count)]


def dot(a, b, contract):
    return lax.dot_general(a, b, (contract, ((), ())), preferred_element_type=F32)


def grads_kernel(
    sizes, info, own_ref, recv_ref, start_ref, end_ref, row_ref, col_ref, panel_ref, err_t
):
    half_pieces, piece, width, col_bits = sizes
    tokens = 2 * half_pieces * piece
    acts = []
    for index in range(2 * half_pieces):
        source = own_ref if index < half_pieces else recv_ref
        both = source[index % half_pieces, 0]
        acts.append(both[:, :width])
        err_t[:, index * piece : (index + 1) * piece] = both[:, width:].astype(F32).T
    act = jnp.concatenate(acts, axis=0)
    lane = lax.broadcasted_iota(jnp.int32, (1, tokens), 1)
    place = lane // piece
    position = lane % piece
    for k in range(col_bits):
        mine = (info[2] >> (col_bits - 1 - k)) & 1
        position = position + (mine ^ ((place >> k) & 1)) * (tokens >> (col_bits - k))
    member = (position >= start_ref[0]) & (position < end_ref[0])
    captions = member.shape[0]

    def fill(out_ref, first):
        for group in range(out_ref.shape[1] // (8 * width)):
            base = first + group * 8
            if not isinstance(base, int):
                base = pl.multiple_of(base, 8)
            rows = err_t[pl.ds(base, 8), :]
            weighted = [
                jnp.where(member, rows[k : k + 1, :], 0.0).astype(BF16) for k in range(8)
            ]
            summed = dot(jnp.concatenate(weighted, axis=0), act, ((1,), (0,)))
            for k in range(8):
                column = (group * 8 + k) * width
                out_ref[:, column : column + width] = summed[
                    k * captions : (k + 1) * captions
                ].astype(BF16)

    fill(row_ref, info[4])
    fill(col_ref, info[5])
    fill(panel_ref, 0)


def all_grads(info, own, recv, starts, ends, half_rows, tile_cols, stop, width, col_bits):
    half_pieces, groups, piece, both = own.shape
    captions = starts.shape[1]
    sizes = (half_pieces, piece, width, col_bits)
    pieces = pl.BlockSpec((half_pieces, 1, piece, both), lambda a, info: (0, a, 0, 0))
    bounds = pl.BlockSpec((1, captions, 1), lambda a, info: (a, 0, 0))
    outs = [half_rows, tile_cols, stop]
    total = sum(outs) // width
    return pl.pallas_call(
        functools.partial(grads_kernel, sizes),
        grid_spec=pltpu.PrefetchScalarGridSpec(
            num_scalar_prefetch=1,
            grid=(groups,),
            in_specs=[pieces, pieces, bounds, bounds],
            out_specs=[pl.BlockSpec((captions, n), lambda a, info: (a, 0)) for n in outs],
            scratch_shapes=[pltpu.VMEM((width, 2 * half_pieces * piece), F32)],
        ),
        out_shape=[jax.ShapeDtypeStruct((groups * captions, n), BF16) for n in outs],
        cost_estimate=pl.CostEstimate(
            flops=4 * groups * total * captions * 2 * half_pieces * piece * width,
            bytes_accessed=2 * own.size * 2 + 2 * groups * captions * sum(outs),
            transcendentals=0,
        ),
        name="grads",
    )(info, own, recv, starts, ends)


def row_panel_kernel(sizes, info, inverse_ref, panel_grads, row_grads, *refs):
    chunks, options, rows, pivot_rows, scale = sizes
    sources = refs[: chunks * options]
    out_ref, pivot_ref, held, sem = refs[chunks * options :]
    width = inverse_ref.shape[1]
    step = rows // chunks
    turn = pl.program_id(0)

    def target(chunk):
        extra = pivot_rows if chunk == chunks - 1 else 0
        return held.at[pl.ds(chunk * step, step + extra)]

    def wait(chunk):
        pltpu.make_async_copy(sources[chunk * options], target(chunk), sem.at[chunk]).wait()

    @pl.when(turn == 0)
    def _():
        for chunk in reversed(range(chunks)):
            for option in range(options):

                @pl.when(info[3] == option)
                def _():
                    pltpu.make_async_copy(
                        sources[chunk * options + option], target(chunk), sem.at[chunk]
                    ).start()

        wait(chunks - 1)
        grads = panel_grads[...]
        packed = held[rows : rows + pivot_rows, :]
        pivot = jnp.concatenate([packed[:, :width], packed[:, width:]], axis=0).astype(F32)
        pivot = pivot + scale * dot(grads[:, width:], grads[:, :width], ((0,), (0,)))
        pivot = dot(pivot.astype(BF16), inverse_ref[0], ((1,), (1,))).astype(BF16)
        pivot_ref[...] = pivot

    for chunk in range(chunks - 1):

        @pl.when(turn == chunk)
        def _():
            wait(chunk)

    at = pl.multiple_of(turn * step, step)
    mine = row_grads[...].T
    start = held[pl.ds(at, step), :].astype(F32)
    both = start + scale * dot(mine, panel_grads[...], ((1,), (0,)))
    first = dot(both[:, :width].astype(BF16), inverse_ref[0], ((1,), (1,))).astype(BF16)
    second = both[:, width:] - dot(first, pivot_ref[...], ((1,), (1,)))
    second = dot(second.astype(BF16), inverse_ref[1], ((1,), (1,)))
    ids = info[6] + at + lax.broadcasted_iota(jnp.int32, second.shape, 0)
    out_ref[:, :width] = first
    out_ref[:, width : 2 * width] = jnp.where(ids >= width, second, 0.0).astype(BF16)
    out_ref[:, 2 * width :] = mine


def row_panel(info, inverse, panel_grads, row_grads, pieces, scale):
    chunks, options = len(pieces), len(pieces[0])
    captions, rows = row_grads.shape
    stop = panel_grads.shape[1]
    width = stop // 2
    step = rows // chunks
    pivot_rows = pieces[-1][0].shape[0] - pieces[0][0].shape[0]
    whole = pl.BlockSpec(memory_space=pltpu.VMEM)
    return pl.pallas_call(
        functools.partial(row_panel_kernel, (chunks, options, rows, pivot_rows, scale)),
        grid=(chunks,),
        in_specs=[
            pl.BlockSpec(memory_space=pltpu.SMEM),
            whole,
            whole,
            pl.BlockSpec((captions, step), lambda s: (0, s)),
        ]
        + [pl.BlockSpec(memory_space=pl.ANY)] * (chunks * options),
        out_specs=[
            pl.BlockSpec((step, stop + captions), lambda s: (s, 0)),
            pl.BlockSpec((width, width), lambda s: (0, 0)),
        ],
        out_shape=[
            jax.ShapeDtypeStruct((rows, stop + captions), BF16),
            jax.ShapeDtypeStruct((width, width), BF16),
        ],
        scratch_shapes=[
            pltpu.VMEM((rows + pivot_rows, stop), BF16),
            pltpu.SemaphoreType.DMA((chunks,)),
        ],
        cost_estimate=pl.CostEstimate(
            flops=2 * rows * (stop * captions + 3 * width * width),
            bytes_accessed=4 * rows * stop + 2 * captions * (rows + stop),
            transcendentals=0,
        ),
        name="row_panel",
    )(info, inverse, panel_grads, row_grads, *[p for piece in pieces for p in piece])


def col_panel_kernel(sizes, info, inverse_ref, pivot_ref, panel_grads, col_grads, *refs):
    chunks, options, scale = sizes
    sources = refs[: chunks * options]
    out_ref, held, sem = refs[chunks * options :]
    width = inverse_ref.shape[1]
    step = out_ref.shape[1] // chunks

    def target(chunk):
        return held.at[:, pl.ds(chunk * step, step)]

    for chunk in range(chunks):
        for option in range(options):

            @pl.when(info[1] == option)
            def _():
                pltpu.make_async_copy(
                    sources[chunk * options + option], target(chunk), sem.at[chunk]
                ).start()

    grads = panel_grads[...]
    first_inverse, second_inverse = inverse_ref[0], inverse_ref[1]
    for chunk in range(chunks):
        pltpu.make_async_copy(sources[chunk * options], target(chunk), sem.at[chunk]).wait()

    mine = col_grads[...]
    both = held[...].astype(F32) + scale * dot(grads, mine, ((0,), (0,)))
    first = dot(first_inverse, both[:width].astype(BF16), ((1,), (0,))).astype(BF16)
    second = both[width:] - dot(pivot_ref[...], first, ((1,), (0,)))
    second = dot(second_inverse, second.astype(BF16), ((1,), (0,))).astype(BF16)
    out_ref[:width] = -first
    out_ref[width : 2 * width] = -second
    out_ref[2 * width :] = (mine.astype(F32) * scale).astype(BF16)


def col_panel(info, inverse, pivot, panel_grads, col_grads, pieces, first_col, scale):
    chunks, options = len(pieces), len(pieces[0])
    stop, step = pieces[0][0].shape
    captions = col_grads.shape[0]
    width = stop // 2
    whole = pl.BlockSpec(memory_space=pltpu.VMEM)
    columns = chunks * step
    return pl.pallas_call(
        functools.partial(col_panel_kernel, (chunks, options, scale)),
        grid=(1,),
        in_specs=[pl.BlockSpec(memory_space=pltpu.SMEM)]
        + [whole] * 3
        + [pl.BlockSpec((captions, columns), lambda s: (0, first_col // columns))]
        + [pl.BlockSpec(memory_space=pl.ANY)] * (chunks * options),
        out_specs=whole,
        out_shape=jax.ShapeDtypeStruct((stop + captions, columns), BF16),
        scratch_shapes=[
            pltpu.VMEM((stop, columns), BF16),
            pltpu.SemaphoreType.DMA((chunks,)),
        ],
        cost_estimate=pl.CostEstimate(
            flops=2 * columns * (stop * captions + 3 * width * width),
            bytes_accessed=4 * columns * stop + 2 * captions * (columns + stop),
            transcendentals=0,
        ),
        name="col_panel",
    )(info, inverse, pivot, panel_grads, col_grads, *[p for piece in pieces for p in piece])


def update_kernel(sizes, info, mine, other, right, ridge_ref, *refs):
    first_col, stop, base, blocks = sizes
    out_ref = refs[-1]
    step = pl.program_id(0) + base
    block, columns = out_ref.shape
    inside = max(0, min(columns, stop - first_col))

    def write(left):
        which = step // blocks
        row = info[7] + ((info[0] ^ which) * blocks + step - which * blocks) * block
        panel_part = jnp.logical_and(info[2] == 0, inside > 0)

        @pl.when(jnp.logical_and(row >= stop, jnp.logical_not(panel_part & (inside == columns))))
        def _():
            out_ref[...] = ridge_ref[...] + dot(left[...], right[...], ((1,), (0,)))

        @pl.when(row < stop)
        def _():
            out_ref[...] = jnp.zeros_like(out_ref)

        if inside:

            @pl.when(panel_part)
            def _():
                out_ref[:, :inside] = left[:, first_col : first_col + inside].astype(F32)

    @pl.when(step < blocks)
    def _():
        write(mine)

    @pl.when(step >= blocks)
    def _():
        write(other)


def update(info, out, mine, other, right, ridge, first_col, stop, halves):
    depth, columns = right.shape
    half_rows = mine.shape[0]
    block = min(ROW_BLOCK, half_rows)
    blocks = half_rows // block
    at = first_col // columns
    assert at * columns == first_col and stop % block == 0

    base = halves[0] * blocks

    def rows_of(step, info):
        which = (step + base) // blocks
        return (info[0] ^ which) * blocks + step + base - which * blocks

    tile = pl.BlockSpec((block, columns), lambda s, i: (rows_of(s, i), at))
    specs = [
        pl.BlockSpec((block, depth), lambda s, i: (jnp.minimum(s + base, blocks - 1), 0)),
        pl.BlockSpec((block, depth), lambda s, i: (jnp.maximum(s + base - blocks, 0), 0)),
        pl.BlockSpec((depth, columns), lambda s, i: (0, 0)),
        tile,
    ]
    operands = [mine, other, right, ridge]
    aliases = {}
    if out is not None:
        specs.append(pl.BlockSpec(memory_space=pl.ANY))
        operands.append(out)
        aliases = {len(operands): 0}
    rows = len(halves) * half_rows
    return pl.pallas_call(
        functools.partial(update_kernel, (first_col, stop, base, blocks)),
        grid_spec=pltpu.PrefetchScalarGridSpec(
            num_scalar_prefetch=1, grid=(len(halves) * blocks,), in_specs=specs, out_specs=tile
        ),
        out_shape=jax.ShapeDtypeStruct(ridge.shape, F32),
        input_output_aliases=aliases,
        cost_estimate=pl.CostEstimate(
            flops=2 * rows * columns * depth,
            bytes_accessed=8 * rows * columns + 2 * depth * (rows + columns),
            transcendentals=0,
        ),
        name="update",
    )(info, *operands)


def chunk_kernel(boxes, who, info, ridge_ref, *refs):
    count = len(boxes)
    wide, narrow, in_sem, out_sem = refs[-4:]
    outs = refs[-4 - count : -4]
    extra = refs[0] if len(refs) > count + 4 else None
    rows, columns = wide.shape[1:]

    @pl.when(info[who] == 0)
    def _():
        loads, stores = [], []
        for k, (row, column) in enumerate(boxes):
            source = ridge_ref.at[pl.ds(row, rows), pl.ds(column, columns)]
            loads.append([pltpu.make_async_copy(source, wide.at[k], in_sem.at[k])])
            if extra is not None:
                target = narrow.at[k, pl.ds(rows, outs[k].shape[0] - rows)]
                loads[k].append(pltpu.make_async_copy(extra, target, in_sem.at[count + k]))
            for load in loads[k]:
                load.start()
        for k in range(count):
            for load in loads[k]:
                load.wait()
            narrow[k, :rows] = wide[k].astype(BF16)
            stores.append(pltpu.make_async_copy(narrow.at[k], outs[k], out_sem.at[k]))
            stores[k].start()
        for store in stores:
            store.wait()


def chunks_of(info, ridge, boxes, shape, who, extra=None):
    count = len(boxes)
    rows, columns = shape
    total = rows + (0 if extra is None else extra.shape[0])
    place = pl.BlockSpec(memory_space=pl.ANY)
    operands = [ridge] if extra is None else [ridge, extra]
    return pl.pallas_call(
        functools.partial(chunk_kernel, boxes, who),
        in_specs=[pl.BlockSpec(memory_space=pltpu.SMEM)] + [place] * len(operands),
        out_specs=[place] * count,
        out_shape=[jax.ShapeDtypeStruct((total, columns), BF16)] * count,
        scratch_shapes=[
            pltpu.VMEM((count, rows, columns), F32),
            pltpu.VMEM((count, total, columns), BF16),
            pltpu.SemaphoreType.DMA((2 * count,)),
            pltpu.SemaphoreType.DMA((count,)),
        ],
        cost_estimate=pl.CostEstimate(
            flops=0, bytes_accessed=6 * count * rows * columns, transcendentals=0
        ),
        name="chunks",
    )(info, *operands)


def gray_order(count):
    forward = [i ^ (i >> 1) for i in range(count)]
    return forward, [forward[0]] + forward[:0:-1]


def per_device(activations, errors, act_proj, err_proj, lengths, ridge, pivot_inverse):
    col_count, row_count = lax.axis_size("col"), lax.axis_size("row")
    col_idx, row_idx = lax.axis_index("col"), lax.axis_index("row")
    core = col_idx & 1
    tile_rows, tile_cols = ridge.shape
    half_rows = tile_rows // 2
    width = pivot_inverse.shape[1]
    stop = 2 * width
    proj_width = act_proj.shape[1]
    captions = lengths.shape[1]
    scale = 1.0 / (captions * row_count)
    inverse = pivot_inverse.astype(BF16)

    pairs = col_count // 2
    orders = gray_order(pairs)
    depth = jnp.int32(0)
    for c, order in enumerate(orders):
        for d, pair in enumerate(order):
            depth = jnp.where(col_idx == 2 * pair + c, d, depth)

    row_err = (row_idx * tile_rows + core * half_rows) // proj_width
    col_err = (col_idx * tile_cols) // proj_width
    facts = [
        core,
        row_idx,
        col_idx,
        depth,
        row_err,
        col_err,
        row_idx * tile_rows + core * half_rows,
        row_idx * tile_rows,
    ]
    slot = jnp.arange(len(facts), dtype=jnp.int32)
    info = jnp.zeros_like(slot)
    for k, fact in enumerate(facts):
        info = jnp.where(slot == k, fact, info)

    boxes = [(width, 0), (width + width // 2, 0)]
    pivot = chunks_of(info, ridge, boxes, (width // 2, width), 2)
    pivot = jnp.concatenate(pivot, axis=1)
    sent = []
    for z in range(1, row_count):
        sent.append(lax.ppermute(pivot, ("row", "col"), [(0, z * col_count)]))
    pivot = jnp.where(row_idx == 0, pivot, functools.reduce(jnp.add, sent))

    line_step = tile_cols // LINE_CHUNKS
    steps = LINE_CHUNKS + CHAINS * (row_count - 2)
    arrived, source, first = [], [], []
    for ns in (range(CHAINS), range(CHAINS, LINE_CHUNKS)):
        boxes = [(0, n * line_step) for n in ns]
        first += chunks_of(info, ridge, boxes, (stop, line_step), 1)
    for k in range(steps):
        if k >= LINE_CHUNKS:
            piece = arrived[k - CHAINS]
        elif k >= CHAINS:
            piece = jnp.where(row_idx == 0, first[k], arrived[k - CHAINS])
        else:
            piece = first[k]
        source.append(piece)
        arrived.append(lax.ppermute(piece, "row", [(z - 1, z) for z in range(1, row_count)]))
    line = [
        [source[n]] + [arrived[n + CHAINS * (z - 1)] for z in range(1, row_count)]
        for n in range(LINE_CHUNKS)
    ]

    plane_step = half_rows // PLANE_CHUNKS
    plane = []
    last = PLANE_CHUNKS - 1
    made = {}
    for name, ns in (("a", (0,)), ("b", tuple(range(1, last))), ("c", (last,))):
        boxes = [(half_rows + n * plane_step, 0) for n in ns]
        boxes += [(n * plane_step, 0) for n in ns]
        extra = pivot if name == "c" else None
        got = chunks_of(info, ridge, boxes, (plane_step, stop), 2, extra)
        for k, n in enumerate(ns):
            made[n] = (got[k], got[len(ns) + k])
    for n in range(PLANE_CHUNKS):
        other, own = made[n]
        other = lax.ppermute(other, "col", [(0, 1)])
        hops = [jnp.where(col_idx == 1, other, own)]
        for d in range(1, pairs):
            perm = [(2 * o[d - 1] + c, 2 * o[d] + c) for c, o in enumerate(orders)]
            hops.append(lax.ppermute(hops[-1], "col", perm))
        plane.append(hops)

    all_lengths = lengths
    for k in range(row_count.bit_length() - 1):
        got = lax.ppermute(all_lengths, "row", xor_pairs(row_count, 1 << k))
        all_lengths = jnp.concatenate([all_lengths, got], axis=0)
    before = jnp.arange(captions)[:, None] < jnp.arange(captions)[None, :]
    starts = jnp.sum(jnp.where(before[None], all_lengths[:, :, None], 0), axis=1)
    ends = (starts + all_lengths)[:, :, None]
    starts = starts[:, :, None]

    total = jnp.concatenate(
        [
            jnp.dot(activations, act_proj, preferred_element_type=F32),
            jnp.dot(errors, err_proj, preferred_element_type=F32),
        ],
        axis=1,
    )
    col_bits = col_count.bit_length() - 1
    for k in range(col_bits):
        half = total.shape[0] // 2
        upper = ((col_idx >> k) & 1) == 1
        low, high = total[:half], total[half:]
        send = jnp.where(upper, low, high)
        keep = jnp.where(upper, high, low)
        got = lax.ppermute(send, "col", xor_pairs(col_count, 1 << k))
        total = keep + got
    held = total.astype(BF16)[None, None]
    for k in range(row_count.bit_length() - 1):
        got = lax.ppermute(held, "row", xor_pairs(row_count, 1 << k))
        held = jnp.concatenate([held, got], axis=1)
    for k in reversed(range(col_bits)):
        got = lax.ppermute(held, "col", xor_pairs(col_count, 1 << k))
        if k:
            held = jnp.concatenate([held, got], axis=0)

    row_grads, col_grads, panel_grads = all_grads(
        info, held, got, starts, ends, half_rows, tile_cols, stop, proj_width, col_bits
    )
    mine, pivot_panel = row_panel(info, inverse, panel_grads, row_grads, plane, scale)
    other = lax.ppermute(mine, "col", xor_pairs(col_count, 1))

    out = None
    for index, call in enumerate(CALLS):
        first_col = call[0] * line_step
        pieces = [line[n] for n in call]
        right = col_panel(
            info,
            inverse,
            pivot_panel,
            panel_grads,
            col_grads,
            pieces,
            first_col,
            scale,
        )
        for halves in SPLITS[index]:
            rest = other if 1 in halves else mine
            out = update(info, out, mine, rest, right, ridge, first_col, stop, halves)
    return out


def solution(mesh):
    in_specs = (
        P("row", "col"),
        P("row", "col"),
        P("col", None),
        P("col", None),
        P("row", None),
        P("row", "col"),
        P(),
    )

    return jax.shard_map(
        per_device, mesh=mesh, in_specs=in_specs, out_specs=P("row", "col"), check_vma=False
    )
```

```python
import functools

import jax
import jax.numpy as jnp
from jax import lax
from jax.experimental import pallas as pl
from jax.experimental.pallas import tpu as pltpu
from jax.sharding import PartitionSpec as P


BF16 = jnp.bfloat16
F32 = jnp.float32
PLANE_CHUNKS = 4
LINE_CHUNKS = 8
CHAINS = 2
CALLS = ((0, 1, 2, 3), (4, 5, 6, 7))
UPDATES = (((0,), (0,)), ((1,), (0,)), ((0, 1), (1,)))
PIVOT_CHUNK = 2
PLANE_GROUPS = ((0,), (1, 3), (2,))
LINE_GROUPS = ((0, 1), (2, 3), (4, 5, 6, 7))
ROW_BLOCK = 512


def xor_pairs(count, bit):
    return [(i, i ^ bit) for i in range(count)]


def dot(a, b, contract):
    return lax.dot_general(a, b, (contract, ((), ())), preferred_element_type=F32)


def grads_kernel(sizes, info, own_ref, recv_ref, row_ref, col_ref, panel_ref, err_t):
    half_pieces, piece, width, col_bits, captions = sizes
    tokens = 2 * half_pieces * piece
    acts = []
    for index in range(2 * half_pieces):
        source = own_ref if index < half_pieces else recv_ref
        both = source[index % half_pieces, 0, :piece]
        acts.append(both[:, :width])
        err_t[:, index * piece : (index + 1) * piece] = both[:, width:].astype(F32).T
    act = jnp.concatenate(acts, axis=0)
    lengths = own_ref[0, 0, piece:, :captions]
    first = lax.broadcasted_iota(jnp.int32, (captions, captions), 0)
    second = lax.broadcasted_iota(jnp.int32, (captions, captions), 1)
    start = dot((second < first).astype(BF16), lengths, ((1,), (1,)))[:, :1].astype(jnp.int32)
    end = dot((second <= first).astype(BF16), lengths, ((1,), (1,)))[:, :1].astype(jnp.int32)
    lane = lax.broadcasted_iota(jnp.int32, (1, tokens), 1)
    place = lane // piece
    position = lane % piece
    for k in range(col_bits):
        mine = (info[2] >> (col_bits - 1 - k)) & 1
        position = position + (mine ^ ((place >> k) & 1)) * (tokens >> (col_bits - k))
    member = (position >= start) & (position < end)

    def fill(out_ref, first):
        for group in range(out_ref.shape[1] // (8 * width)):
            base = first + group * 8
            if not isinstance(base, int):
                base = pl.multiple_of(base, 8)
            rows = err_t[pl.ds(base, 8), :]
            weighted = [
                jnp.where(member, rows[k : k + 1, :], 0.0).astype(BF16) for k in range(8)
            ]
            summed = dot(jnp.concatenate(weighted, axis=0), act, ((1,), (0,)))
            for k in range(8):
                column = (group * 8 + k) * width
                out_ref[:, column : column + width] = summed[
                    k * captions : (k + 1) * captions
                ].astype(BF16)

    fill(row_ref, info[4])
    fill(col_ref, info[5])
    fill(panel_ref, 0)


def all_grads(info, own, recv, captions, piece, half_rows, tile_cols, stop, width, col_bits):
    half_pieces, groups, rows, both = own.shape
    sizes = (half_pieces, piece, width, col_bits, captions)
    pieces = pl.BlockSpec((half_pieces, 1, rows, both), lambda a, info: (0, a, 0, 0))
    outs = [half_rows, tile_cols, stop]
    total = sum(outs) // width
    return pl.pallas_call(
        functools.partial(grads_kernel, sizes),
        grid_spec=pltpu.PrefetchScalarGridSpec(
            num_scalar_prefetch=1,
            grid=(groups,),
            in_specs=[pieces, pieces],
            out_specs=[pl.BlockSpec((captions, n), lambda a, info: (a, 0)) for n in outs],
            scratch_shapes=[pltpu.VMEM((width, 2 * half_pieces * piece), F32)],
        ),
        out_shape=[jax.ShapeDtypeStruct((groups * captions, n), BF16) for n in outs],
        cost_estimate=pl.CostEstimate(
            flops=4 * groups * total * captions * 2 * half_pieces * piece * width,
            bytes_accessed=2 * own.size * 2 + 2 * groups * captions * sum(outs),
            transcendentals=0,
        ),
        name="grads",
    )(info, own, recv)


def pivot_kernel(options, scale, info, inverse_ref, panel_grads, *refs):
    sources = refs[:options]
    pivot_ref, short_ref, held, sem = refs[options:]
    width = inverse_ref.shape[1]
    tail = held.shape[0]
    rows = sources[0].shape[0] - tail
    for option, source in enumerate(sources):

        @pl.when(info[3] == option)
        def _():
            pltpu.make_async_copy(source.at[pl.ds(rows, tail)], held, sem).start()

    short_ref[...] = inverse_ref[...].astype(BF16)
    grads = panel_grads[...]
    gram = dot(grads[:, width:], grads[:, :width], ((0,), (0,)))
    pltpu.make_async_copy(sources[0].at[pl.ds(rows, tail)], held, sem).wait()
    pivot = jnp.concatenate([held[:, :width], held[:, width:]], axis=0).astype(F32)
    pivot = (pivot + scale * gram).astype(BF16)
    pivot_ref[...] = dot(pivot, short_ref[0], ((1,), (1,))).astype(BF16)


def pivot_panel(info, inverse, panel_grads, pieces, scale):
    stop = panel_grads.shape[1]
    width = stop // 2
    whole = pl.BlockSpec(memory_space=pltpu.VMEM)
    return pl.pallas_call(
        functools.partial(pivot_kernel, len(pieces), scale),
        in_specs=[pl.BlockSpec(memory_space=pltpu.SMEM), whole, whole]
        + [pl.BlockSpec(memory_space=pl.ANY)] * len(pieces),
        out_specs=[whole, whole],
        out_shape=[
            jax.ShapeDtypeStruct((width, width), BF16),
            jax.ShapeDtypeStruct((2, width, width), BF16),
        ],
        scratch_shapes=[pltpu.VMEM((width // 2, stop), BF16), pltpu.SemaphoreType.DMA],
        cost_estimate=pl.CostEstimate(
            flops=4 * width**3, bytes_accessed=16 * width * width, transcendentals=0
        ),
        name="pivot",
    )(info, inverse, panel_grads, *pieces)


def row_panel_kernel(sizes, info, inverse_ref, pivot_ref, panel_grads, row_grads, *refs):
    chunks, options, scale = sizes
    sources = refs[: chunks * options]
    out_ref, held, sem = refs[chunks * options :]
    width = inverse_ref.shape[1]
    step = held.shape[0] // chunks
    turn = pl.program_id(0)

    def copy(chunk, option):
        source = sources[chunk * options + option].at[pl.ds(0, step)]
        return pltpu.make_async_copy(source, held.at[pl.ds(chunk * step, step)], sem.at[chunk])

    @pl.when(turn == 0)
    def _():
        for chunk in range(chunks):
            for option in range(options):

                @pl.when(info[3] == option)
                def _():
                    copy(chunk, option).start()

    for chunk in range(chunks):

        @pl.when(turn == chunk)
        def _():
            copy(chunk, 0).wait()

    at = pl.multiple_of(turn * step, step)
    mine = row_grads[...].T
    start = held[pl.ds(at, step), :].astype(F32)
    both = start + scale * dot(mine, panel_grads[...], ((1,), (0,)))
    first = dot(both[:, :width].astype(BF16), inverse_ref[0], ((1,), (1,))).astype(BF16)
    second = both[:, width:] - dot(first, pivot_ref[...], ((1,), (1,)))
    second = dot(second.astype(BF16), inverse_ref[1], ((1,), (1,)))
    ids = info[6] + at + lax.broadcasted_iota(jnp.int32, second.shape, 0)
    out_ref[:, :width] = first
    out_ref[:, width : 2 * width] = jnp.where(ids >= width, second, 0.0).astype(BF16)
    out_ref[:, 2 * width :] = mine


def row_panel(info, inverse, pivot, panel_grads, row_grads, pieces, scale):
    chunks, options = len(pieces), len(pieces[0])
    captions, rows = row_grads.shape
    stop = panel_grads.shape[1]
    width = stop // 2
    step = rows // chunks
    whole = pl.BlockSpec(memory_space=pltpu.VMEM)
    return pl.pallas_call(
        functools.partial(row_panel_kernel, (chunks, options, scale)),
        grid=(chunks,),
        in_specs=[
            pl.BlockSpec(memory_space=pltpu.SMEM),
            whole,
            whole,
            whole,
            pl.BlockSpec((captions, step), lambda s: (0, s)),
        ]
        + [pl.BlockSpec(memory_space=pl.ANY)] * (chunks * options),
        out_specs=pl.BlockSpec((step, stop + captions), lambda s: (s, 0)),
        out_shape=jax.ShapeDtypeStruct((rows, stop + captions), BF16),
        scratch_shapes=[pltpu.VMEM((rows, stop), BF16), pltpu.SemaphoreType.DMA((chunks,))],
        cost_estimate=pl.CostEstimate(
            flops=2 * rows * (stop * captions + 3 * width * width),
            bytes_accessed=4 * rows * stop + 2 * captions * (rows + stop),
            transcendentals=0,
        ),
        name="row_panel",
    )(info, inverse, pivot, panel_grads, row_grads, *[p for piece in pieces for p in piece])


def col_panel_kernel(sizes, info, inverse_ref, pivot_ref, panel_grads, col_grads, *refs):
    chunks, options, scale = sizes
    sources = refs[: chunks * options]
    out_ref, held, sem = refs[chunks * options :]
    width = inverse_ref.shape[1]
    step = out_ref.shape[1] // chunks

    def target(chunk):
        return held.at[:, pl.ds(chunk * step, step)]

    for chunk in range(chunks):
        for option in range(options):

            @pl.when(info[1] == option)
            def _():
                pltpu.make_async_copy(
                    sources[chunk * options + option], target(chunk), sem.at[chunk]
                ).start()

    grads = panel_grads[...]
    first_inverse, second_inverse = inverse_ref[0], inverse_ref[1]
    for chunk in range(chunks):
        pltpu.make_async_copy(sources[chunk * options], target(chunk), sem.at[chunk]).wait()

    mine = col_grads[...]
    both = held[...].astype(F32) + scale * dot(grads, mine, ((0,), (0,)))
    first = dot(first_inverse, both[:width].astype(BF16), ((1,), (0,))).astype(BF16)
    second = both[width:] - dot(pivot_ref[...], first, ((1,), (0,)))
    second = dot(second_inverse, second.astype(BF16), ((1,), (0,))).astype(BF16)
    out_ref[:width] = -first
    out_ref[width : 2 * width] = -second
    out_ref[2 * width :] = (mine.astype(F32) * scale).astype(BF16)


def col_panel(info, inverse, pivot, panel_grads, col_grads, pieces, first_col, scale):
    chunks, options = len(pieces), len(pieces[0])
    stop, step = pieces[0][0].shape
    captions = col_grads.shape[0]
    width = stop // 2
    whole = pl.BlockSpec(memory_space=pltpu.VMEM)
    columns = chunks * step
    return pl.pallas_call(
        functools.partial(col_panel_kernel, (chunks, options, scale)),
        grid=(1,),
        in_specs=[pl.BlockSpec(memory_space=pltpu.SMEM)]
        + [whole] * 3
        + [pl.BlockSpec((captions, columns), lambda s: (0, first_col // columns))]
        + [pl.BlockSpec(memory_space=pl.ANY)] * (chunks * options),
        out_specs=whole,
        out_shape=jax.ShapeDtypeStruct((stop + captions, columns), BF16),
        scratch_shapes=[
            pltpu.VMEM((stop, columns), BF16),
            pltpu.SemaphoreType.DMA((chunks,)),
        ],
        cost_estimate=pl.CostEstimate(
            flops=2 * columns * (stop * captions + 3 * width * width),
            bytes_accessed=4 * columns * stop + 2 * captions * (columns + stop),
            transcendentals=0,
        ),
        name="col_panel",
    )(info, inverse, pivot, panel_grads, col_grads, *[p for piece in pieces for p in piece])


def update_kernel(sizes, info, mine, other, *refs):
    parts, stop, base, blocks, first_col = sizes
    rights = refs[:parts]
    ridge_ref, out_ref = refs[parts], refs[-1]
    step = pl.program_id(0) + base
    block = out_ref.shape[0]

    def write(left):
        which = step // blocks
        row = info[7] + ((info[0] ^ which) * blocks + step - which * blocks) * block
        holds = info[2] == 0

        @pl.when(row < stop)
        def _():
            out_ref[...] = jnp.zeros_like(out_ref)

        at = 0
        for right in rights:
            until = at + right.shape[1]
            busy = row >= stop
            if first_col + until <= stop:
                busy = busy & jnp.logical_not(holds)

            @pl.when(busy)
            def _():
                product = dot(left[...], right[...], ((1,), (0,)))
                out_ref[:, at:until] = ridge_ref[:, at:until] + product

            at = until

        inside = min(stop - first_col, out_ref.shape[1])
        if inside > 0:

            @pl.when(holds)
            def _():
                out_ref[:, :inside] = left[:, first_col : first_col + inside].astype(F32)

    @pl.when(step < blocks)
    def _():
        write(mine)

    @pl.when(step >= blocks)
    def _():
        write(other)


def update(info, out, mine, other, rights, ridge, stop, halves, first_col):
    depth = mine.shape[1]
    columns = sum(right.shape[1] for right in rights)
    at = first_col // columns
    half_rows = mine.shape[0]
    block = min(ROW_BLOCK, half_rows)
    blocks = half_rows // block
    assert stop % block == 0 and at * columns == first_col
    base = halves[0] * blocks

    def rows_of(step, info):
        which = (step + base) // blocks
        return (info[0] ^ which) * blocks + step + base - which * blocks

    tile = pl.BlockSpec((block, columns), lambda s, i: (rows_of(s, i), at))
    specs = [
        pl.BlockSpec((block, depth), lambda s, i: (jnp.minimum(s + base, blocks - 1), 0)),
        pl.BlockSpec((block, depth), lambda s, i: (jnp.maximum(s + base - blocks, 0), 0)),
    ]
    specs += [pl.BlockSpec(right.shape, lambda s, i: (0, 0)) for right in rights]
    specs.append(tile)
    operands = [mine, other, *rights, ridge]
    aliases = {}
    if out is not None:
        specs.append(pl.BlockSpec(memory_space=pl.ANY))
        operands.append(out)
        aliases = {len(operands): 0}
    rows = len(halves) * half_rows
    return pl.pallas_call(
        functools.partial(update_kernel, (len(rights), stop, base, blocks, first_col)),
        grid_spec=pltpu.PrefetchScalarGridSpec(
            num_scalar_prefetch=1,
            grid=(len(halves) * blocks,),
            in_specs=specs,
            out_specs=tile,
        ),
        out_shape=jax.ShapeDtypeStruct(ridge.shape, F32),
        input_output_aliases=aliases,
        cost_estimate=pl.CostEstimate(
            flops=2 * rows * columns * depth,
            bytes_accessed=8 * rows * columns + 2 * depth * (rows + columns),
            transcendentals=0,
        ),
        name="update",
    )(info, *operands)


def chunk_kernel(boxes, who, dead, choices, info, ridge_ref, *refs):
    count = len(boxes)
    wide, narrow, in_sem, out_sem = refs[-4:]
    outs = refs[-4 - count : -4]
    extras = refs[: len(refs) - count - 4]
    extras = [extras[k : k + choices] for k in range(0, len(extras), choices)]
    rows, columns = wide.shape[1:]

    idle = jnp.logical_and(info[2] == 0, dead)

    @pl.when((info[who] == 0) & jnp.logical_not(idle))
    def _():
        loads, stores = [], []
        for k, (row, column) in enumerate(boxes):
            source = ridge_ref.at[pl.ds(row, rows), pl.ds(column, columns)]
            loads.append([pltpu.make_async_copy(source, wide.at[k], in_sem.at[k])])
            loads[k][0].start()
            tail = outs[k].shape[0] - rows
            part = extras[0][0].shape[1] if extras else 0
            for index, options in enumerate(extras):
                for side in range(2):
                    target = narrow.at[
                        k,
                        pl.ds(rows, tail),
                        pl.ds(side * columns // 2 + index * part, part),
                    ]
                    sem = in_sem.at[count + (2 * index + side) * count + k]
                    for z, option in enumerate(options):
                        source = option.at[pl.ds(side * tail, tail)]
                        load = pltpu.make_async_copy(source, target, sem)

                        @pl.when(info[1] == z)
                        def _():
                            load.start()

                    loads[k].append(load)
        for k in range(count):
            for load in loads[k]:
                load.wait()
            narrow[k, :rows] = wide[k].astype(BF16)
            stores.append(pltpu.make_async_copy(narrow.at[k], outs[k], out_sem.at[k]))
            stores[k].start()
        for store in stores:
            store.wait()


def chunks_of(info, ridge, boxes, shape, who, extras=(), dead=False):
    count = len(boxes)
    rows, columns = shape
    total = rows + (columns // 4 if extras else 0)
    choices = len(extras[0]) if extras else 1
    place = pl.BlockSpec(memory_space=pl.ANY)
    operands = [ridge, *[piece for options in extras for piece in options]]
    return pl.pallas_call(
        functools.partial(chunk_kernel, boxes, who, dead, choices),
        in_specs=[pl.BlockSpec(memory_space=pltpu.SMEM)] + [place] * len(operands),
        out_specs=[place] * count,
        out_shape=[jax.ShapeDtypeStruct((total, columns), BF16)] * count,
        scratch_shapes=[
            pltpu.VMEM((count, rows, columns), F32),
            pltpu.VMEM((count, total, columns), BF16),
            pltpu.SemaphoreType.DMA(((1 + 2 * len(extras)) * count,)),
            pltpu.SemaphoreType.DMA((count,)),
        ],
        cost_estimate=pl.CostEstimate(
            flops=0, bytes_accessed=6 * count * rows * columns, transcendentals=0
        ),
        name="chunks",
    )(info, *operands)


def gray_order(count):
    forward = [i ^ (i >> 1) for i in range(count)]
    return forward, [forward[0]] + forward[:0:-1]


def per_device(activations, errors, act_proj, err_proj, lengths, ridge, pivot_inverse):
    col_count, row_count = lax.axis_size("col"), lax.axis_size("row")
    col_idx, row_idx = lax.axis_index("col"), lax.axis_index("row")
    core = col_idx & 1
    tile_rows, tile_cols = ridge.shape
    half_rows = tile_rows // 2
    width = pivot_inverse.shape[1]
    stop = 2 * width
    proj_width = act_proj.shape[1]
    captions = lengths.shape[1]
    scale = 1.0 / (captions * row_count)

    pairs = col_count // 2
    orders = gray_order(pairs)
    depth = jnp.int32(0)
    for c, order in enumerate(orders):
        for d, pair in enumerate(order):
            depth = jnp.where(col_idx == 2 * pair + c, d, depth)

    row_err = (row_idx * tile_rows + core * half_rows) // proj_width
    col_err = (col_idx * tile_cols) // proj_width
    facts = [
        core,
        row_idx,
        col_idx,
        depth,
        row_err,
        col_err,
        row_idx * tile_rows + core * half_rows,
        row_idx * tile_rows,
    ]
    slot = jnp.arange(len(facts), dtype=jnp.int32)
    info = jnp.zeros_like(slot)
    for k, fact in enumerate(facts):
        info = jnp.where(slot == k, fact, info)

    pivots = list(chunks_of(info, ridge, [(width, 0)], (width, width), 2))
    for z in range(1, row_count):
        pivots.append(lax.ppermute(pivots[0], ("row", "col"), [(0, z * col_count)]))

    line_step = tile_cols // LINE_CHUNKS
    steps = LINE_CHUNKS + CHAINS * (row_count - 2)
    arrived, source, first = [], [], []
    for ks in LINE_GROUPS:
        boxes = [(0, k * line_step) for k in ks]
        dead = (max(ks) + 1) * line_step <= stop
        first += chunks_of(info, ridge, boxes, (stop, line_step), 1, (), dead)
    for k in range(steps):
        if k >= LINE_CHUNKS:
            piece = arrived[k - CHAINS]
        elif k >= CHAINS:
            piece = jnp.where(row_idx == 0, first[k], arrived[k - CHAINS])
        else:
            piece = first[k]
        source.append(piece)
        arrived.append(lax.ppermute(piece, "row", [(z - 1, z) for z in range(1, row_count)]))
    line = [
        [source[n]] + [arrived[n + CHAINS * (z - 1)] for z in range(1, row_count)]
        for n in range(LINE_CHUNKS)
    ]

    plane_step = half_rows // PLANE_CHUNKS
    plane, made = [], {}
    for ns in PLANE_GROUPS:
        boxes = [(half_rows + n * plane_step, 0) for n in ns]
        boxes += [(n * plane_step, 0) for n in ns]
        extras = [pivots] if PIVOT_CHUNK in ns else ()
        got = chunks_of(info, ridge, boxes, (plane_step, stop), 2, extras)
        for k, n in enumerate(ns):
            made[n] = (got[k], got[len(ns) + k])
    for n in range(PLANE_CHUNKS):
        other, own = made[n]
        other = lax.ppermute(other, "col", [(0, 1)])
        hops = [jnp.where(col_idx == 1, other, own)]
        for d in range(1, pairs):
            perm = [(2 * o[d - 1] + c, 2 * o[d] + c) for c, o in enumerate(orders)]
            hops.append(lax.ppermute(hops[-1], "col", perm))
        plane.append(hops)

    total = jnp.concatenate(
        [
            jnp.dot(activations, act_proj, preferred_element_type=F32),
            jnp.dot(errors, err_proj, preferred_element_type=F32),
        ],
        axis=1,
    )
    col_bits = col_count.bit_length() - 1
    for k in range(col_bits):
        half = total.shape[0] // 2
        upper = ((col_idx >> k) & 1) == 1
        low, high = total[:half], total[half:]
        send = jnp.where(upper, low, high)
        keep = jnp.where(upper, high, low)
        got = lax.ppermute(send, "col", xor_pairs(col_count, 1 << k))
        total = keep + got
    piece = total.shape[0]
    counts = jnp.pad(lengths.astype(F32), ((0, 15), (0, total.shape[1] - captions)))
    held = jnp.concatenate([total, counts], axis=0).astype(BF16)[None, None]
    for k in range(row_count.bit_length() - 1):
        got = lax.ppermute(held, "row", xor_pairs(row_count, 1 << k))
        held = jnp.concatenate([held, got], axis=1)
    for k in reversed(range(col_bits)):
        got = lax.ppermute(held, "col", xor_pairs(col_count, 1 << k))
        if k:
            held = jnp.concatenate([held, got], axis=0)

    row_grads, col_grads, panel_grads = all_grads(
        info, held, got, captions, piece, half_rows, tile_cols, stop, proj_width, col_bits
    )
    pivot, inverse = pivot_panel(
        info, pivot_inverse, panel_grads, plane[PIVOT_CHUNK], scale
    )
    mine = row_panel(info, inverse, pivot, panel_grads, row_grads, plane, scale)
    other = lax.ppermute(mine, "col", xor_pairs(col_count, 1))
    rights = []
    for call in CALLS:
        pieces = [line[n] for n in call]
        first_col = call[0] * line_step
        rights.append(
            col_panel(
                info, inverse, pivot, panel_grads, col_grads, pieces, first_col, scale
            )
        )
    out = None
    for halves, parts in UPDATES:
        rest = other if 1 in halves else mine
        used = [rights[part] for part in parts]
        first_col = CALLS[parts[0]][0] * line_step
        out = update(info, out, mine, rest, used, ridge, stop, halves, first_col)
    return out


def solution(mesh):
    in_specs = (
        P("row", "col"),
        P("row", "col"),
        P("col", None),
        P("col", None),
        P("row", None),
        P("row", "col"),
        P(),
    )

    return jax.shard_map(
        per_device, mesh=mesh, in_specs=in_specs, out_specs=P("row", "col"), check_vma=False
    )
```

```python
import functools

import jax
import jax.numpy as jnp
from jax import lax
from jax.experimental import pallas as pl
from jax.experimental.pallas import tpu as pltpu
from jax.sharding import PartitionSpec as P


BF16 = jnp.bfloat16
F32 = jnp.float32
PLANE_CHUNKS = 4
LINE_CHUNKS = 8
CHAINS = 2
CALLS = ((0, 1, 2, 3), (4, 5, 6, 7))
UPDATES = (((0, 0),), ((1, 0), (0, 1), (1, 1)))
PIVOT_CHUNK = 3
PLANE_GROUPS = ((0,), (1, 2), (3,))
LINE_GROUPS = ((0, 1), (2, 3), (4, 5, 6, 7))
ROW_BLOCK = 512


def xor_pairs(count, bit):
    return [(i, i ^ bit) for i in range(count)]


def dot(a, b, contract):
    return lax.dot_general(a, b, (contract, ((), ())), preferred_element_type=F32)


def grads_kernel(sizes, info, own_ref, recv_ref, row_ref, col_ref, panel_ref, err_t):
    half_pieces, piece, width, col_bits, captions = sizes
    tokens = 2 * half_pieces * piece
    acts = []
    for index in range(2 * half_pieces):
        source = own_ref if index < half_pieces else recv_ref
        both = source[index % half_pieces, 0, :piece]
        acts.append(both[:, :width])
        err_t[:, index * piece : (index + 1) * piece] = both[:, width:].astype(F32).T
    act = jnp.concatenate(acts, axis=0)
    lengths = own_ref[0, 0, piece:, :captions]
    first = lax.broadcasted_iota(jnp.int32, (captions, captions), 0)
    second = lax.broadcasted_iota(jnp.int32, (captions, captions), 1)
    start = dot((second < first).astype(BF16), lengths, ((1,), (1,)))[:, :1].astype(jnp.int32)
    end = dot((second <= first).astype(BF16), lengths, ((1,), (1,)))[:, :1].astype(jnp.int32)
    lane = lax.broadcasted_iota(jnp.int32, (1, tokens), 1)
    place = lane // piece
    position = lane % piece
    for k in range(col_bits):
        mine = (info[2] >> (col_bits - 1 - k)) & 1
        position = position + (mine ^ ((place >> k) & 1)) * (tokens >> (col_bits - k))
    member = (position >= start) & (position < end)

    def fill(out_ref, first):
        for group in range(out_ref.shape[1] // (8 * width)):
            base = first + group * 8
            if not isinstance(base, int):
                base = pl.multiple_of(base, 8)
            rows = err_t[pl.ds(base, 8), :]
            weighted = [
                jnp.where(member, rows[k : k + 1, :], 0.0).astype(BF16) for k in range(8)
            ]
            summed = dot(jnp.concatenate(weighted, axis=0), act, ((1,), (0,)))
            for k in range(8):
                column = (group * 8 + k) * width
                out_ref[:, column : column + width] = summed[
                    k * captions : (k + 1) * captions
                ].astype(BF16)

    fill(row_ref, info[4])
    fill(col_ref, info[5])
    fill(panel_ref, 0)


def all_grads(info, own, recv, captions, piece, half_rows, tile_cols, stop, width, col_bits):
    half_pieces, groups, rows, both = own.shape
    sizes = (half_pieces, piece, width, col_bits, captions)
    pieces = pl.BlockSpec((half_pieces, 1, rows, both), lambda a, info: (0, a, 0, 0))
    outs = [half_rows, tile_cols, stop]
    total = sum(outs) // width
    return pl.pallas_call(
        functools.partial(grads_kernel, sizes),
        grid_spec=pltpu.PrefetchScalarGridSpec(
            num_scalar_prefetch=1,
            grid=(groups,),
            in_specs=[pieces, pieces],
            out_specs=[pl.BlockSpec((captions, n), lambda a, info: (a, 0)) for n in outs],
            scratch_shapes=[pltpu.VMEM((width, 2 * half_pieces * piece), F32)],
        ),
        out_shape=[jax.ShapeDtypeStruct((groups * captions, n), BF16) for n in outs],
        cost_estimate=pl.CostEstimate(
            flops=4 * groups * total * captions * 2 * half_pieces * piece * width,
            bytes_accessed=2 * own.size * 2 + 2 * groups * captions * sum(outs),
            transcendentals=0,
        ),
        name="grads",
    )(info, own, recv)


def pivot_kernel(options, scale, info, inverse_ref, panel_grads, *refs):
    sources = refs[:options]
    pivot_ref, short_ref, held, sem = refs[options:]
    width = inverse_ref.shape[1]
    tail = held.shape[0]
    rows = sources[0].shape[0] - tail
    for option, source in enumerate(sources):

        @pl.when(info[3] == option)
        def _():
            pltpu.make_async_copy(source.at[pl.ds(rows, tail)], held, sem).start()

    short_ref[...] = inverse_ref[...].astype(BF16)
    grads = panel_grads[...]
    gram = dot(grads[:, width:], grads[:, :width], ((0,), (0,)))
    pltpu.make_async_copy(sources[0].at[pl.ds(rows, tail)], held, sem).wait()
    pivot = jnp.concatenate([held[:, :width], held[:, width:]], axis=0).astype(F32)
    pivot = (pivot + scale * gram).astype(BF16)
    pivot_ref[...] = dot(pivot, short_ref[0], ((1,), (1,))).astype(BF16)


def pivot_panel(info, inverse, panel_grads, pieces, scale):
    stop = panel_grads.shape[1]
    width = stop // 2
    whole = pl.BlockSpec(memory_space=pltpu.VMEM)
    return pl.pallas_call(
        functools.partial(pivot_kernel, len(pieces), scale),
        in_specs=[pl.BlockSpec(memory_space=pltpu.SMEM), whole, whole]
        + [pl.BlockSpec(memory_space=pl.ANY)] * len(pieces),
        out_specs=[whole, whole],
        out_shape=[
            jax.ShapeDtypeStruct((width, width), BF16),
            jax.ShapeDtypeStruct((2, width, width), BF16),
        ],
        scratch_shapes=[pltpu.VMEM((width // 2, stop), BF16), pltpu.SemaphoreType.DMA],
        cost_estimate=pl.CostEstimate(
            flops=4 * width**3, bytes_accessed=16 * width * width, transcendentals=0
        ),
        name="pivot",
    )(info, inverse, panel_grads, *pieces)


def row_panel_kernel(sizes, info, inverse_ref, pivot_ref, panel_grads, row_grads, *refs):
    chunks, options, scale = sizes
    sources = refs[: chunks * options]
    out_ref, held, sem = refs[chunks * options :]
    width = inverse_ref.shape[1]
    step = held.shape[0] // chunks
    turn = pl.program_id(0)

    def copy(chunk, option):
        source = sources[chunk * options + option].at[pl.ds(0, step)]
        return pltpu.make_async_copy(source, held.at[pl.ds(chunk * step, step)], sem.at[chunk])

    @pl.when(turn == 0)
    def _():
        for chunk in range(chunks):
            for option in range(options):

                @pl.when(info[3] == option)
                def _():
                    copy(chunk, option).start()

    for chunk in range(chunks):

        @pl.when(turn == chunk)
        def _():
            copy(chunk, 0).wait()

    at = pl.multiple_of(turn * step, step)
    mine = row_grads[...].T
    start = held[pl.ds(at, step), :].astype(F32)
    both = start + scale * dot(mine, panel_grads[...], ((1,), (0,)))
    first = dot(both[:, :width].astype(BF16), inverse_ref[0], ((1,), (1,))).astype(BF16)
    second = both[:, width:] - dot(first, pivot_ref[...], ((1,), (1,)))
    second = dot(second.astype(BF16), inverse_ref[1], ((1,), (1,)))
    ids = info[6] + at + lax.broadcasted_iota(jnp.int32, second.shape, 0)
    out_ref[:, :width] = first
    out_ref[:, width : 2 * width] = jnp.where(ids >= width, second, 0.0).astype(BF16)
    out_ref[:, 2 * width :] = mine


def row_panel(info, inverse, pivot, panel_grads, row_grads, pieces, scale):
    chunks, options = len(pieces), len(pieces[0])
    captions, rows = row_grads.shape
    stop = panel_grads.shape[1]
    width = stop // 2
    step = rows // chunks
    whole = pl.BlockSpec(memory_space=pltpu.VMEM)
    return pl.pallas_call(
        functools.partial(row_panel_kernel, (chunks, options, scale)),
        grid=(chunks,),
        in_specs=[
            pl.BlockSpec(memory_space=pltpu.SMEM),
            whole,
            whole,
            whole,
            pl.BlockSpec((captions, step), lambda s: (0, s)),
        ]
        + [pl.BlockSpec(memory_space=pl.ANY)] * (chunks * options),
        out_specs=pl.BlockSpec((step, stop + captions), lambda s: (s, 0)),
        out_shape=jax.ShapeDtypeStruct((rows, stop + captions), BF16),
        scratch_shapes=[pltpu.VMEM((rows, stop), BF16), pltpu.SemaphoreType.DMA((chunks,))],
        cost_estimate=pl.CostEstimate(
            flops=2 * rows * (stop * captions + 3 * width * width),
            bytes_accessed=4 * rows * stop + 2 * captions * (rows + stop),
            transcendentals=0,
        ),
        name="row_panel",
    )(info, inverse, pivot, panel_grads, row_grads, *[p for piece in pieces for p in piece])


def col_panel_kernel(sizes, info, inverse_ref, pivot_ref, panel_grads, col_grads, *refs):
    chunks, options, scale = sizes
    sources = refs[: chunks * options]
    out_ref, held, sem = refs[chunks * options :]
    width = inverse_ref.shape[1]
    step = out_ref.shape[1] // chunks

    def target(chunk):
        return held.at[:, pl.ds(chunk * step, step)]

    for chunk in range(chunks):
        for option in range(options):

            @pl.when(info[1] == option)
            def _():
                pltpu.make_async_copy(
                    sources[chunk * options + option], target(chunk), sem.at[chunk]
                ).start()

    grads = panel_grads[...]
    first_inverse, second_inverse = inverse_ref[0], inverse_ref[1]
    for chunk in range(chunks):
        pltpu.make_async_copy(sources[chunk * options], target(chunk), sem.at[chunk]).wait()

    mine = col_grads[...]
    both = held[...].astype(F32) + scale * dot(grads, mine, ((0,), (0,)))
    first = dot(first_inverse, both[:width].astype(BF16), ((1,), (0,))).astype(BF16)
    second = both[width:] - dot(pivot_ref[...], first, ((1,), (0,)))
    second = dot(second_inverse, second.astype(BF16), ((1,), (0,))).astype(BF16)
    out_ref[:width] = -first
    out_ref[width : 2 * width] = -second
    out_ref[2 * width :] = (mine.astype(F32) * scale).astype(BF16)


def col_panel(info, inverse, pivot, panel_grads, col_grads, pieces, first_col, scale):
    chunks, options = len(pieces), len(pieces[0])
    stop, step = pieces[0][0].shape
    captions = col_grads.shape[0]
    width = stop // 2
    whole = pl.BlockSpec(memory_space=pltpu.VMEM)
    columns = chunks * step
    return pl.pallas_call(
        functools.partial(col_panel_kernel, (chunks, options, scale)),
        grid=(1,),
        in_specs=[pl.BlockSpec(memory_space=pltpu.SMEM)]
        + [whole] * 3
        + [pl.BlockSpec((captions, columns), lambda s: (0, first_col // columns))]
        + [pl.BlockSpec(memory_space=pl.ANY)] * (chunks * options),
        out_specs=whole,
        out_shape=jax.ShapeDtypeStruct((stop + captions, columns), BF16),
        scratch_shapes=[
            pltpu.VMEM((stop, columns), BF16),
            pltpu.SemaphoreType.DMA((chunks,)),
        ],
        cost_estimate=pl.CostEstimate(
            flops=2 * columns * (stop * captions + 3 * width * width),
            bytes_accessed=4 * columns * stop + 2 * captions * (columns + stop),
            transcendentals=0,
        ),
        name="col_panel",
    )(info, inverse, pivot, panel_grads, col_grads, *[p for piece in pieces for p in piece])


def pick(step, values):
    value = jnp.int32(values[0])
    for k in range(1, len(values)):
        value = jnp.where(step == k, values[k], value)
    return value


def update_kernel(sizes, info, mine, other, *refs):
    work, parts, stop, blocks = sizes
    rights = refs[: len(parts)]
    ridge_ref, out_ref = refs[len(parts)], refs[-1]
    step = pl.program_id(0)
    block, columns = out_ref.shape
    segment = step // blocks
    holds = info[2] == 0

    for place, (half, part) in enumerate(work):
        left, right = (mine, other)[half], rights[parts.index(part)]
        first_col = part * columns
        inside = max(0, min(stop - first_col, columns))
        row = info[7] + ((info[0] ^ half) * blocks + step - place * blocks) * block
        now = segment == place
        busy = now & (row >= stop)
        if inside == columns:
            busy = busy & jnp.logical_not(holds)

        @pl.when(busy)
        def _():
            out_ref[...] = ridge_ref[...] + dot(left[...], right[...], ((1,), (0,)))

        @pl.when(now & (row < stop))
        def _():
            out_ref[...] = jnp.zeros_like(out_ref)

        if inside:

            @pl.when(now & holds)
            def _():
                out_ref[:, :inside] = left[:, first_col : first_col + inside].astype(F32)


def update(info, out, mine, other, rights, ridge, stop, work):
    parts = sorted({part for _, part in work})
    depth, columns = rights[parts[0]].shape
    half_rows = mine.shape[0]
    block = min(ROW_BLOCK, half_rows)
    blocks = half_rows // block
    assert stop % block == 0

    def half_of(step):
        return pick(step // blocks, [half for half, _ in work])

    def tile_of(step, info):
        part = pick(step // blocks, [part for _, part in work])
        return (info[0] ^ half_of(step)) * blocks + step % blocks, part

    def left_of(half):
        return lambda step, info: (jnp.where(half_of(step) == half, step % blocks, 0), 0)

    specs = [pl.BlockSpec((block, depth), left_of(half)) for half in range(2)]
    specs += [pl.BlockSpec((depth, columns), lambda s, i: (0, 0)) for _ in parts]
    specs.append(pl.BlockSpec((block, columns), tile_of))
    operands = [mine, other, *[rights[part] for part in parts], ridge]
    aliases = {}
    if out is not None:
        specs.append(pl.BlockSpec(memory_space=pl.ANY))
        operands.append(out)
        aliases = {len(operands): 0}
    rows = len(work) * half_rows
    return pl.pallas_call(
        functools.partial(update_kernel, (work, parts, stop, blocks)),
        grid_spec=pltpu.PrefetchScalarGridSpec(
            num_scalar_prefetch=1,
            grid=(len(work) * blocks,),
            in_specs=specs,
            out_specs=pl.BlockSpec((block, columns), tile_of),
        ),
        out_shape=jax.ShapeDtypeStruct(ridge.shape, F32),
        input_output_aliases=aliases,
        cost_estimate=pl.CostEstimate(
            flops=2 * rows * columns * depth,
            bytes_accessed=8 * rows * columns + 2 * depth * (rows + columns),
            transcendentals=0,
        ),
        name="update",
    )(info, *operands)


def chunk_kernel(boxes, who, dead, choices, info, ridge_ref, *refs):
    count = len(boxes)
    wide, narrow, in_sem, out_sem = refs[-4:]
    outs = refs[-4 - count : -4]
    extras = refs[: len(refs) - count - 4]
    extras = [extras[k : k + choices] for k in range(0, len(extras), choices)]
    rows, columns = wide.shape[1:]

    ready = info[who[0]] == 0
    for place in who[1:]:
        ready = ready & (info[place] == 0)
    if dead:
        ready = ready & (info[2] != 0)

    @pl.when(ready)
    def _():
        loads, stores = [], []
        for k, (row, column) in enumerate(boxes):
            source = ridge_ref.at[pl.ds(row, rows), pl.ds(column, columns)]
            loads.append([pltpu.make_async_copy(source, wide.at[k], in_sem.at[k])])
            loads[k][0].start()
            tail = outs[k].shape[0] - rows
            part = extras[0][0].shape[1] if extras else 0
            for index, options in enumerate(extras):
                for side in range(2):
                    target = narrow.at[
                        k,
                        pl.ds(rows, tail),
                        pl.ds(side * columns // 2 + index * part, part),
                    ]
                    sem = in_sem.at[count + (2 * index + side) * count + k]
                    for z, option in enumerate(options):
                        source = option.at[pl.ds(side * tail, tail)]
                        load = pltpu.make_async_copy(source, target, sem)

                        @pl.when(info[1] == z)
                        def _():
                            load.start()

                    loads[k].append(load)
        for k in range(count):
            for load in loads[k]:
                load.wait()
            narrow[k, :rows] = wide[k].astype(BF16)
            stores.append(pltpu.make_async_copy(narrow.at[k], outs[k], out_sem.at[k]))
            stores[k].start()
        for store in stores:
            store.wait()


def chunks_of(info, ridge, boxes, shape, who, extras=(), dead=False):
    count = len(boxes)
    rows, columns = shape
    total = rows + (columns // 4 if extras else 0)
    choices = len(extras[0]) if extras else 1
    place = pl.BlockSpec(memory_space=pl.ANY)
    operands = [ridge, *[piece for options in extras for piece in options]]
    return pl.pallas_call(
        functools.partial(chunk_kernel, boxes, who, dead, choices),
        in_specs=[pl.BlockSpec(memory_space=pltpu.SMEM)] + [place] * len(operands),
        out_specs=[place] * count,
        out_shape=[jax.ShapeDtypeStruct((total, columns), BF16)] * count,
        scratch_shapes=[
            pltpu.VMEM((count, rows, columns), F32),
            pltpu.VMEM((count, total, columns), BF16),
            pltpu.SemaphoreType.DMA(((1 + 2 * len(extras)) * count,)),
            pltpu.SemaphoreType.DMA((count,)),
        ],
        cost_estimate=pl.CostEstimate(
            flops=0, bytes_accessed=6 * count * rows * columns, transcendentals=0
        ),
        name="chunks",
    )(info, *operands)


def gray_order(count):
    forward = [i ^ (i >> 1) for i in range(count)]
    return forward, [forward[0]] + forward[:0:-1]


def per_device(activations, errors, act_proj, err_proj, lengths, ridge, pivot_inverse):
    col_count, row_count = lax.axis_size("col"), lax.axis_size("row")
    col_idx, row_idx = lax.axis_index("col"), lax.axis_index("row")
    core = col_idx & 1
    tile_rows, tile_cols = ridge.shape
    half_rows = tile_rows // 2
    width = pivot_inverse.shape[1]
    stop = 2 * width
    proj_width = act_proj.shape[1]
    captions = lengths.shape[1]
    scale = 1.0 / (captions * row_count)

    pairs = col_count // 2
    orders = gray_order(pairs)
    depth = jnp.int32(0)
    for c, order in enumerate(orders):
        for d, pair in enumerate(order):
            depth = jnp.where(col_idx == 2 * pair + c, d, depth)

    row_err = (row_idx * tile_rows + core * half_rows) // proj_width
    col_err = (col_idx * tile_cols) // proj_width
    facts = [
        core,
        row_idx,
        col_idx,
        depth,
        row_err,
        col_err,
        row_idx * tile_rows + core * half_rows,
        row_idx * tile_rows,
    ]
    slot = jnp.arange(len(facts), dtype=jnp.int32)
    info = jnp.zeros_like(slot)
    for k, fact in enumerate(facts):
        info = jnp.where(slot == k, fact, info)

    pivots = list(chunks_of(info, ridge, [(width, 0)], (width, width), (1, 2)))
    for z in range(1, row_count):
        pivots.append(lax.ppermute(pivots[0], ("row", "col"), [(0, z * col_count)]))

    line_step = tile_cols // LINE_CHUNKS
    steps = LINE_CHUNKS + CHAINS * (row_count - 2)
    arrived, source, first = [], [], []
    for ks in LINE_GROUPS:
        boxes = [(0, k * line_step) for k in ks]
        dead = (max(ks) + 1) * line_step <= stop
        first += chunks_of(info, ridge, boxes, (stop, line_step), (1,), (), dead)
    for k in range(steps):
        if k >= LINE_CHUNKS:
            piece = arrived[k - CHAINS]
        elif k >= CHAINS:
            piece = jnp.where(row_idx == 0, first[k], arrived[k - CHAINS])
        else:
            piece = first[k]
        source.append(piece)
        arrived.append(lax.ppermute(piece, "row", [(z - 1, z) for z in range(1, row_count)]))
    line = [
        [source[n]] + [arrived[n + CHAINS * (z - 1)] for z in range(1, row_count)]
        for n in range(LINE_CHUNKS)
    ]

    plane_step = half_rows // PLANE_CHUNKS
    plane, made = [], {}
    for ns in PLANE_GROUPS:
        boxes = [(half_rows + n * plane_step, 0) for n in ns]
        boxes += [(n * plane_step, 0) for n in ns]
        extras = [pivots] if PIVOT_CHUNK in ns else ()
        got = chunks_of(info, ridge, boxes, (plane_step, stop), (2,), extras)
        for k, n in enumerate(ns):
            made[n] = (got[k], got[len(ns) + k])
    for n in range(PLANE_CHUNKS):
        other, own = made[n]
        other = lax.ppermute(other, "col", [(0, 1)])
        hops = [jnp.where(col_idx == 1, other, own)]
        for d in range(1, pairs):
            perm = [(2 * o[d - 1] + c, 2 * o[d] + c) for c, o in enumerate(orders)]
            hops.append(lax.ppermute(hops[-1], "col", perm))
        plane.append(hops)

    total = jnp.concatenate(
        [
            jnp.dot(activations, act_proj, preferred_element_type=F32),
            jnp.dot(errors, err_proj, preferred_element_type=F32),
        ],
        axis=1,
    )
    col_bits = col_count.bit_length() - 1
    for k in range(col_bits):
        half = total.shape[0] // 2
        upper = ((col_idx >> k) & 1) == 1
        low, high = total[:half], total[half:]
        send = jnp.where(upper, low, high)
        keep = jnp.where(upper, high, low)
        got = lax.ppermute(send, "col", xor_pairs(col_count, 1 << k))
        total = keep + got
    piece = total.shape[0]
    counts = jnp.pad(lengths.astype(F32), ((0, 15), (0, total.shape[1] - captions)))
    held = jnp.concatenate([total, counts], axis=0).astype(BF16)[None, None]
    for k in range(row_count.bit_length() - 1):
        got = lax.ppermute(held, "row", xor_pairs(row_count, 1 << k))
        held = jnp.concatenate([held, got], axis=1)
    for k in reversed(range(col_bits)):
        got = lax.ppermute(held, "col", xor_pairs(col_count, 1 << k))
        if k:
            held = jnp.concatenate([held, got], axis=0)

    row_grads, col_grads, panel_grads = all_grads(
        info, held, got, captions, piece, half_rows, tile_cols, stop, proj_width, col_bits
    )
    pivot, inverse = pivot_panel(
        info, pivot_inverse, panel_grads, plane[PIVOT_CHUNK], scale
    )
    mine = row_panel(info, inverse, pivot, panel_grads, row_grads, plane, scale)
    other = lax.ppermute(mine, "col", xor_pairs(col_count, 1))
    rights = []
    for call in CALLS:
        pieces = [line[n] for n in call]
        first_col = call[0] * line_step
        rights.append(
            col_panel(
                info, inverse, pivot, panel_grads, col_grads, pieces, first_col, scale
            )
        )
    out = None
    for work in UPDATES:
        rest = other if any(half for half, _ in work) else mine
        out = update(info, out, mine, rest, rights, ridge, stop, work)
    return out


def solution(mesh):
    in_specs = (
        P("row", "col"),
        P("row", "col"),
        P("col", None),
        P("col", None),
        P("row", None),
        P("row", "col"),
        P(),
    )

    return jax.shard_map(
        per_device, mesh=mesh, in_specs=in_specs, out_specs=P("row", "col"), check_vma=False
    )
```

```python
import functools

import jax
import jax.numpy as jnp
from jax import lax
from jax.experimental import pallas as pl
from jax.experimental.pallas import tpu as pltpu
from jax.sharding import PartitionSpec as P


BF16 = jnp.bfloat16
F32 = jnp.float32
PLANE_CHUNKS = 4
LINE_CHUNKS = 8
CHAINS = 2
CALLS = ((0, 1, 2, 3), (4, 5, 6, 7))
UPDATES = (((0, 0),), ((1, 0), (0, 1), (1, 1)))
PIVOT_CHUNK = 3
PLANE_GROUPS = ((0,), (1, 2), (3,))
LINE_GROUPS = ((0, 1), (2, 3), (4, 5, 6, 7))
ROW_BLOCK = 1024
SLABS = 4


def xor_pairs(count, bit):
    return [(i, i ^ bit) for i in range(count)]


def dot(a, b, contract):
    return lax.dot_general(a, b, (contract, ((), ())), preferred_element_type=F32)


def grads_kernel(sizes, info, own_ref, recv_ref, row_ref, col_ref, panel_ref, err_t):
    half_pieces, piece, width, col_bits, captions = sizes
    tokens = 2 * half_pieces * piece
    acts = []
    for index in range(2 * half_pieces):
        source = own_ref if index < half_pieces else recv_ref
        both = source[index % half_pieces, 0, :piece]
        acts.append(both[:, :width])
        err_t[:, index * piece : (index + 1) * piece] = both[:, width:].astype(F32).T
    act = jnp.concatenate(acts, axis=0)
    lengths = own_ref[0, 0, piece:, :captions]
    first = lax.broadcasted_iota(jnp.int32, (captions, captions), 0)
    second = lax.broadcasted_iota(jnp.int32, (captions, captions), 1)
    start = dot((second < first).astype(BF16), lengths, ((1,), (1,)))[:, :1].astype(jnp.int32)
    end = dot((second <= first).astype(BF16), lengths, ((1,), (1,)))[:, :1].astype(jnp.int32)
    lane = lax.broadcasted_iota(jnp.int32, (1, tokens), 1)
    place = lane // piece
    position = lane % piece
    for k in range(col_bits):
        mine = (info[2] >> (col_bits - 1 - k)) & 1
        position = position + (mine ^ ((place >> k) & 1)) * (tokens >> (col_bits - k))
    member = (position >= start) & (position < end)

    def fill(out_ref, first):
        for group in range(out_ref.shape[1] // (8 * width)):
            base = first + group * 8
            if not isinstance(base, int):
                base = pl.multiple_of(base, 8)
            rows = err_t[pl.ds(base, 8), :]
            weighted = [
                jnp.where(member, rows[k : k + 1, :], 0.0).astype(BF16) for k in range(8)
            ]
            summed = dot(jnp.concatenate(weighted, axis=0), act, ((1,), (0,)))
            for k in range(8):
                column = (group * 8 + k) * width
                out_ref[:, column : column + width] = summed[
                    k * captions : (k + 1) * captions
                ].astype(BF16)

    fill(row_ref, info[4])
    fill(col_ref, info[5])
    fill(panel_ref, 0)


def all_grads(info, own, recv, captions, piece, half_rows, tile_cols, stop, width, col_bits):
    half_pieces, groups, rows, both = own.shape
    sizes = (half_pieces, piece, width, col_bits, captions)
    pieces = pl.BlockSpec((half_pieces, 1, rows, both), lambda a, info: (0, a, 0, 0))
    outs = [half_rows, tile_cols, stop]
    total = sum(outs) // width
    return pl.pallas_call(
        functools.partial(grads_kernel, sizes),
        grid_spec=pltpu.PrefetchScalarGridSpec(
            num_scalar_prefetch=1,
            grid=(groups,),
            in_specs=[pieces, pieces],
            out_specs=[pl.BlockSpec((captions, n), lambda a, info: (a, 0)) for n in outs],
            scratch_shapes=[pltpu.VMEM((width, 2 * half_pieces * piece), F32)],
        ),
        out_shape=[jax.ShapeDtypeStruct((groups * captions, n), BF16) for n in outs],
        cost_estimate=pl.CostEstimate(
            flops=4 * groups * total * captions * 2 * half_pieces * piece * width,
            bytes_accessed=2 * own.size * 2 + 2 * groups * captions * sum(outs),
            transcendentals=0,
        ),
        name="grads",
    )(info, own, recv)


def pivot_kernel(options, scale, info, inverse_ref, panel_grads, *refs):
    sources = refs[:options]
    pivot_ref, short_ref, held, sem = refs[options:]
    width = inverse_ref.shape[1]
    tail = held.shape[0]
    rows = sources[0].shape[0] - tail
    for option, source in enumerate(sources):

        @pl.when(info[3] == option)
        def _():
            pltpu.make_async_copy(source.at[pl.ds(rows, tail)], held, sem).start()

    short_ref[...] = inverse_ref[...].astype(BF16)
    grads = panel_grads[...]
    gram = dot(grads[:, width:], grads[:, :width], ((0,), (0,)))
    pltpu.make_async_copy(sources[0].at[pl.ds(rows, tail)], held, sem).wait()
    pivot = jnp.concatenate([held[:, :width], held[:, width:]], axis=0).astype(F32)
    pivot = (pivot + scale * gram).astype(BF16)
    pivot_ref[...] = dot(pivot, short_ref[0], ((1,), (1,))).astype(BF16)


def pivot_panel(info, inverse, panel_grads, pieces, scale):
    stop = panel_grads.shape[1]
    width = stop // 2
    whole = pl.BlockSpec(memory_space=pltpu.VMEM)
    return pl.pallas_call(
        functools.partial(pivot_kernel, len(pieces), scale),
        in_specs=[pl.BlockSpec(memory_space=pltpu.SMEM), whole, whole]
        + [pl.BlockSpec(memory_space=pltpu.HBM)] * len(pieces),
        out_specs=[whole, whole],
        out_shape=[
            jax.ShapeDtypeStruct((width, width), BF16),
            jax.ShapeDtypeStruct((2, width, width), BF16),
        ],
        scratch_shapes=[pltpu.VMEM((width // 2, stop), BF16), pltpu.SemaphoreType.DMA],
        cost_estimate=pl.CostEstimate(
            flops=4 * width**3, bytes_accessed=16 * width * width, transcendentals=0
        ),
        name="pivot",
    )(info, inverse, panel_grads, *pieces)


def row_panel_kernel(sizes, info, inverse_ref, pivot_ref, panel_grads, row_grads, *refs):
    chunks, options, scale = sizes
    sources = refs[: chunks * options]
    out_ref, held, sem = refs[chunks * options :]
    width = inverse_ref.shape[1]
    step = held.shape[0] // chunks
    turn = pl.program_id(0)

    def copy(chunk, option):
        source = sources[chunk * options + option].at[pl.ds(0, step)]
        return pltpu.make_async_copy(source, held.at[pl.ds(chunk * step, step)], sem.at[chunk])

    @pl.when(turn == 0)
    def _():
        for chunk in range(chunks):
            for option in range(options):

                @pl.when(info[3] == option)
                def _():
                    copy(chunk, option).start()

    for chunk in range(chunks):

        @pl.when(turn == chunk)
        def _():
            copy(chunk, 0).wait()

    at = pl.multiple_of(turn * step, step)
    mine = row_grads[...].T
    start = held[pl.ds(at, step), :].astype(F32)
    both = start + scale * dot(mine, panel_grads[...], ((1,), (0,)))
    first = dot(both[:, :width].astype(BF16), inverse_ref[0], ((1,), (1,))).astype(BF16)
    second = both[:, width:] - dot(first, pivot_ref[...], ((1,), (1,)))
    second = dot(second.astype(BF16), inverse_ref[1], ((1,), (1,)))
    ids = info[6] + at + lax.broadcasted_iota(jnp.int32, second.shape, 0)
    out_ref[:, :width] = first
    out_ref[:, width : 2 * width] = jnp.where(ids >= width, second, 0.0).astype(BF16)
    out_ref[:, 2 * width :] = mine


def row_panel(info, inverse, pivot, panel_grads, row_grads, pieces, scale):
    chunks, options = len(pieces), len(pieces[0])
    captions, rows = row_grads.shape
    stop = panel_grads.shape[1]
    width = stop // 2
    step = rows // chunks
    whole = pl.BlockSpec(memory_space=pltpu.VMEM)
    return pl.pallas_call(
        functools.partial(row_panel_kernel, (chunks, options, scale)),
        grid=(chunks,),
        in_specs=[
            pl.BlockSpec(memory_space=pltpu.SMEM),
            whole,
            whole,
            whole,
            pl.BlockSpec((captions, step), lambda s: (0, s)),
        ]
        + [pl.BlockSpec(memory_space=pltpu.HBM)] * (chunks * options),
        out_specs=pl.BlockSpec((step, stop + captions), lambda s: (s, 0)),
        out_shape=jax.ShapeDtypeStruct((rows, stop + captions), BF16),
        scratch_shapes=[pltpu.VMEM((rows, stop), BF16), pltpu.SemaphoreType.DMA((chunks,))],
        cost_estimate=pl.CostEstimate(
            flops=2 * rows * (stop * captions + 3 * width * width),
            bytes_accessed=4 * rows * stop + 2 * captions * (rows + stop),
            transcendentals=0,
        ),
        name="row_panel",
    )(info, inverse, pivot, panel_grads, row_grads, *[p for piece in pieces for p in piece])


def col_panel_kernel(sizes, info, inverse_ref, pivot_ref, panel_grads, col_grads, *refs):
    chunks, options, scale = sizes
    sources = refs[: chunks * options]
    out_ref, held, sem = refs[chunks * options :]
    width = inverse_ref.shape[1]
    step = out_ref.shape[1] // chunks

    def target(chunk):
        return held.at[:, pl.ds(chunk * step, step)]

    for chunk in range(chunks):
        for option in range(options):

            @pl.when(info[1] == option)
            def _():
                pltpu.make_async_copy(
                    sources[chunk * options + option], target(chunk), sem.at[chunk]
                ).start()

    grads = panel_grads[...]
    first_inverse, second_inverse = inverse_ref[0], inverse_ref[1]
    for chunk in range(chunks):
        pltpu.make_async_copy(sources[chunk * options], target(chunk), sem.at[chunk]).wait()

    mine = col_grads[...]
    both = held[...].astype(F32) + scale * dot(grads, mine, ((0,), (0,)))
    first = dot(first_inverse, both[:width].astype(BF16), ((1,), (0,))).astype(BF16)
    second = both[width:] - dot(pivot_ref[...], first, ((1,), (0,)))
    second = dot(second_inverse, second.astype(BF16), ((1,), (0,))).astype(BF16)
    out_ref[:width] = -first
    out_ref[width : 2 * width] = -second
    out_ref[2 * width :] = (mine.astype(F32) * scale).astype(BF16)


def col_panel(info, inverse, pivot, panel_grads, col_grads, pieces, first_col, scale):
    chunks, options = len(pieces), len(pieces[0])
    stop, step = pieces[0][0].shape
    captions = col_grads.shape[0]
    width = stop // 2
    whole = pl.BlockSpec(memory_space=pltpu.VMEM)
    columns = chunks * step
    return pl.pallas_call(
        functools.partial(col_panel_kernel, (chunks, options, scale)),
        grid=(1,),
        in_specs=[pl.BlockSpec(memory_space=pltpu.SMEM)]
        + [whole] * 3
        + [pl.BlockSpec((captions, columns), lambda s: (0, first_col // columns))]
        + [pl.BlockSpec(memory_space=pltpu.HBM)] * (chunks * options),
        out_specs=whole,
        out_shape=jax.ShapeDtypeStruct((stop + captions, columns), BF16),
        scratch_shapes=[
            pltpu.VMEM((stop, columns), BF16),
            pltpu.SemaphoreType.DMA((chunks,)),
        ],
        cost_estimate=pl.CostEstimate(
            flops=2 * columns * (stop * captions + 3 * width * width),
            bytes_accessed=4 * columns * stop + 2 * captions * (columns + stop),
            transcendentals=0,
        ),
        name="col_panel",
    )(info, inverse, pivot, panel_grads, col_grads, *[p for piece in pieces for p in piece])


def pick(step, values):
    value = jnp.int32(values[0])
    for k in range(1, len(values)):
        value = jnp.where(step == k, values[k], value)
    return value


def update_kernel(sizes, info, mine, other, *refs):
    work, parts, stop, blocks = sizes
    rights = refs[: len(parts)]
    ridge_ref, out_ref = refs[len(parts)], refs[-1]
    step = pl.program_id(0)
    block, columns = out_ref.shape
    segment = step // blocks
    holds = info[2] == 0

    for place, (half, part) in enumerate(work):
        left, right = (mine, other)[half], rights[parts.index(part)]
        first_col = part * columns
        inside = max(0, min(stop - first_col, columns))
        row = info[7] + ((info[0] ^ half) * blocks + step - place * blocks) * block
        now = segment == place
        busy = now & (row >= stop)
        if inside == columns:
            busy = busy & jnp.logical_not(holds)

        @pl.when(busy)
        def _():
            out_ref[...] = ridge_ref[...] + dot(left[...], right[...], ((1,), (0,)))

        @pl.when(now & (row < stop))
        def _():
            out_ref[...] = jnp.zeros_like(out_ref)

        if inside:

            @pl.when(now & holds)
            def _():
                out_ref[:, :inside] = left[:, first_col : first_col + inside].astype(F32)


def update(info, out, mine, other, rights, ridge, stop, work):
    parts = sorted({part for _, part in work})
    depth, columns = rights[parts[0]].shape
    half_rows = mine.shape[0]
    block = min(ROW_BLOCK, half_rows)
    blocks = half_rows // block
    assert stop % block == 0

    def half_of(step):
        return pick(step // blocks, [half for half, _ in work])

    def tile_of(step, info):
        part = pick(step // blocks, [part for _, part in work])
        return (info[0] ^ half_of(step)) * blocks + step % blocks, part

    def left_of(half):
        return lambda step, info: (jnp.where(half_of(step) == half, step % blocks, 0), 0)

    specs = [pl.BlockSpec((block, depth), left_of(half)) for half in range(2)]
    specs += [pl.BlockSpec((depth, columns), lambda s, i: (0, 0)) for _ in parts]
    specs.append(pl.BlockSpec((block, columns), tile_of))
    operands = [mine, other, *[rights[part] for part in parts], ridge]
    aliases = {}
    if out is not None:
        specs.append(pl.BlockSpec(memory_space=pl.ANY))
        operands.append(out)
        aliases = {len(operands): 0}
    rows = len(work) * half_rows
    return pl.pallas_call(
        functools.partial(update_kernel, (work, parts, stop, blocks)),
        grid_spec=pltpu.PrefetchScalarGridSpec(
            num_scalar_prefetch=1,
            grid=(len(work) * blocks,),
            in_specs=specs,
            out_specs=pl.BlockSpec((block, columns), tile_of),
        ),
        out_shape=jax.ShapeDtypeStruct(ridge.shape, F32),
        input_output_aliases=aliases,
        cost_estimate=pl.CostEstimate(
            flops=2 * rows * columns * depth,
            bytes_accessed=8 * rows * columns + 2 * depth * (rows + columns),
            transcendentals=0,
        ),
        name="update",
    )(info, *operands)


def chunk_kernel(boxes, who, dead, choices, info, ridge_ref, *refs):
    count = len(boxes)
    wide, narrow, in_sem, out_sem = refs[-4:]
    outs = refs[-4 - count : -4]
    extras = refs[: len(refs) - count - 4]
    extras = [extras[k : k + choices] for k in range(0, len(extras), choices)]
    rows, columns = wide.shape[1:]

    ready = info[who[0]] == 0
    for place in who[1:]:
        ready = ready & (info[place] == 0)
    if dead:
        ready = ready & (info[2] != 0)

    slab = rows // SLABS

    @pl.when(ready)
    def _():
        loads, tails, stores = [], [], []
        for k, (row, column) in enumerate(boxes):
            for q in range(SLABS):
                source = ridge_ref.at[pl.ds(row + q * slab, slab), pl.ds(column, columns)]
                target = wide.at[k, pl.ds(q * slab, slab)]
                loads.append(pltpu.make_async_copy(source, target, in_sem.at[k * SLABS + q]))
                loads[-1].start()
        tail = outs[0].shape[0] - rows
        part = extras[0][0].shape[1] if extras else 0
        used = count * SLABS
        for k in range(count if extras else 0):
            for index, options in enumerate(extras):
                for side in range(2):
                    target = narrow.at[
                        k,
                        pl.ds(rows, tail),
                        pl.ds(side * columns // 2 + index * part, part),
                    ]
                    for z, option in enumerate(options):
                        source = option.at[pl.ds(side * tail, tail)]
                        load = pltpu.make_async_copy(source, target, in_sem.at[used])

                        @pl.when(info[1] == z)
                        def _():
                            load.start()

                    tails.append(load)
                    used = used + 1
        for k in range(count):
            for q in range(SLABS):
                here = pl.ds(q * slab, slab)
                loads[k * SLABS + q].wait()
                narrow[k, q * slab : (q + 1) * slab] = wide[k, q * slab : (q + 1) * slab].astype(BF16)
                sem = out_sem.at[k * SLABS + q]
                stores.append(pltpu.make_async_copy(narrow.at[k, here], outs[k].at[here], sem))
                stores[-1].start()
        for load in tails:
            load.wait()
        for k in range(count if extras else 0):
            here = pl.ds(rows, tail)
            sem = out_sem.at[count * SLABS + k]
            stores.append(pltpu.make_async_copy(narrow.at[k, here], outs[k].at[here], sem))
            stores[-1].start()
        for store in stores:
            store.wait()


def chunks_of(info, ridge, boxes, shape, who, extras=(), dead=False):
    count = len(boxes)
    rows, columns = shape
    total = rows + (columns // 4 if extras else 0)
    choices = len(extras[0]) if extras else 1
    place = pl.BlockSpec(memory_space=pl.ANY)
    operands = [ridge, *[piece for options in extras for piece in options]]
    return pl.pallas_call(
        functools.partial(chunk_kernel, boxes, who, dead, choices),
        in_specs=[pl.BlockSpec(memory_space=pltpu.SMEM)] + [place] * len(operands),
        out_specs=[place] * count,
        out_shape=[jax.ShapeDtypeStruct((total, columns), BF16)] * count,
        scratch_shapes=[
            pltpu.VMEM((count, rows, columns), F32),
            pltpu.VMEM((count, total, columns), BF16),
            pltpu.SemaphoreType.DMA(((SLABS + 2 * len(extras)) * count,)),
            pltpu.SemaphoreType.DMA(((SLABS + 1) * count,)),
        ],
        cost_estimate=pl.CostEstimate(
            flops=0, bytes_accessed=6 * count * rows * columns, transcendentals=0
        ),
        name="chunks",
    )(info, *operands)


def gray_order(count):
    forward = [i ^ (i >> 1) for i in range(count)]
    return forward, [forward[0]] + forward[:0:-1]


def per_device(activations, errors, act_proj, err_proj, lengths, ridge, pivot_inverse):
    col_count, row_count = lax.axis_size("col"), lax.axis_size("row")
    col_idx, row_idx = lax.axis_index("col"), lax.axis_index("row")
    core = col_idx & 1
    tile_rows, tile_cols = ridge.shape
    half_rows = tile_rows // 2
    width = pivot_inverse.shape[1]
    stop = 2 * width
    proj_width = act_proj.shape[1]
    captions = lengths.shape[1]
    scale = 1.0 / (captions * row_count)

    pairs = col_count // 2
    orders = gray_order(pairs)
    depth = jnp.int32(0)
    for c, order in enumerate(orders):
        for d, pair in enumerate(order):
            depth = jnp.where(col_idx == 2 * pair + c, d, depth)

    row_err = (row_idx * tile_rows + core * half_rows) // proj_width
    col_err = (col_idx * tile_cols) // proj_width
    facts = [
        core,
        row_idx,
        col_idx,
        depth,
        row_err,
        col_err,
        row_idx * tile_rows + core * half_rows,
        row_idx * tile_rows,
    ]
    slot = jnp.arange(len(facts), dtype=jnp.int32)
    info = jnp.zeros_like(slot)
    for k, fact in enumerate(facts):
        info = jnp.where(slot == k, fact, info)

    pivots = list(chunks_of(info, ridge, [(width, 0)], (width, width), (1, 2)))
    for z in range(1, row_count):
        pivots.append(lax.ppermute(pivots[0], ("row", "col"), [(0, z * col_count)]))

    line_step = tile_cols // LINE_CHUNKS
    steps = LINE_CHUNKS + CHAINS * (row_count - 2)
    arrived, source, first = [], [], []
    for ks in LINE_GROUPS:
        boxes = [(0, k * line_step) for k in ks]
        dead = (max(ks) + 1) * line_step <= stop
        first += chunks_of(info, ridge, boxes, (stop, line_step), (1,), (), dead)
    for k in range(steps):
        if k >= LINE_CHUNKS:
            piece = arrived[k - CHAINS]
        elif k >= CHAINS:
            piece = jnp.where(row_idx == 0, first[k], arrived[k - CHAINS])
        else:
            piece = first[k]
        source.append(piece)
        arrived.append(lax.ppermute(piece, "row", [(z - 1, z) for z in range(1, row_count)]))
    line = [
        [source[n]] + [arrived[n + CHAINS * (z - 1)] for z in range(1, row_count)]
        for n in range(LINE_CHUNKS)
    ]

    plane_step = half_rows // PLANE_CHUNKS
    plane, made = [], {}
    for ns in PLANE_GROUPS:
        boxes = [(half_rows + n * plane_step, 0) for n in ns]
        boxes += [(n * plane_step, 0) for n in ns]
        extras = [pivots] if PIVOT_CHUNK in ns else ()
        got = chunks_of(info, ridge, boxes, (plane_step, stop), (2,), extras)
        for k, n in enumerate(ns):
            made[n] = (got[k], got[len(ns) + k])
    for n in range(PLANE_CHUNKS):
        other, own = made[n]
        other = lax.ppermute(other, "col", [(0, 1)])
        hops = [jnp.where(col_idx == 1, other, own)]
        for d in range(1, pairs):
            perm = [(2 * o[d - 1] + c, 2 * o[d] + c) for c, o in enumerate(orders)]
            hops.append(lax.ppermute(hops[-1], "col", perm))
        plane.append(hops)

    total = jnp.concatenate(
        [
            jnp.dot(activations, act_proj, preferred_element_type=F32),
            jnp.dot(errors, err_proj, preferred_element_type=F32),
        ],
        axis=1,
    )
    col_bits = col_count.bit_length() - 1
    for k in range(col_bits):
        half = total.shape[0] // 2
        upper = ((col_idx >> k) & 1) == 1
        low, high = total[:half], total[half:]
        send = jnp.where(upper, low, high)
        keep = jnp.where(upper, high, low)
        got = lax.ppermute(send, "col", xor_pairs(col_count, 1 << k))
        total = keep + got
    piece = total.shape[0]
    counts = jnp.pad(lengths.astype(F32), ((0, 15), (0, total.shape[1] - captions)))
    held = jnp.concatenate([total, counts], axis=0).astype(BF16)[None, None]
    for k in range(row_count.bit_length() - 1):
        got = lax.ppermute(held, "row", xor_pairs(row_count, 1 << k))
        held = jnp.concatenate([held, got], axis=1)
    for k in reversed(range(col_bits)):
        got = lax.ppermute(held, "col", xor_pairs(col_count, 1 << k))
        if k:
            held = jnp.concatenate([held, got], axis=0)

    row_grads, col_grads, panel_grads = all_grads(
        info, held, got, captions, piece, half_rows, tile_cols, stop, proj_width, col_bits
    )
    pivot, inverse = pivot_panel(
        info, pivot_inverse, panel_grads, plane[PIVOT_CHUNK], scale
    )
    mine = row_panel(info, inverse, pivot, panel_grads, row_grads, plane, scale)
    other = lax.ppermute(mine, "col", xor_pairs(col_count, 1))
    rights = []
    for call in CALLS:
        pieces = [line[n] for n in call]
        first_col = call[0] * line_step
        rights.append(
            col_panel(
                info, inverse, pivot, panel_grads, col_grads, pieces, first_col, scale
            )
        )
    out = None
    for work in UPDATES:
        rest = other if any(half for half, _ in work) else mine
        out = update(info, out, mine, rest, rights, ridge, stop, work)
    return out


def solution(mesh):
    in_specs = (
        P("row", "col"),
        P("row", "col"),
        P("col", None),
        P("col", None),
        P("row", None),
        P("row", "col"),
        P(),
    )

    return jax.shard_map(
        per_device, mesh=mesh, in_specs=in_specs, out_specs=P("row", "col"), check_vma=False
    )
```
